32 devices in a mesh: tile: 4 (over y, x), mom: 2 (over core), ewin: 4 (over z).
Axes of the slice: x: 2, y: 2, z: 4, core: 2. Of those that a mesh axis runs over, the one named last changes fastest.
Arguments:
- green_ret: bfloat16 [2, 4, 4, 512, 1024], P('mom', 'ewin', 'tile'), may hold values from -0.25 to 0.25
- injection: float32 [2, 4, 4, 512], P('mom', 'ewin', 'tile'), may hold values from 0.1 to 1
- mom_shift: int32 [4], replicated, may hold values from 0 to 7, as said below
- phon_off: int32 [8], replicated, may hold values from -4 to 4
- coupling: float32 [4, 8], replicated, may hold values from 0.05 to 1
- tile_nbr: int32 [4, 4], replicated, may hold values from 0 to 3
Outputs:
- sigma_less: bfloat16 [2, 4, 4, 512, 1024], P('mom', 'ewin', None, 'tile')
The draws below stay inside these ranges and needn't reach their ends.
Inputs may be any that keep to these rules, and one draw needn't show every extreme that they name: `mom_shift`: every residue from 0 to 1 appears among the 4 shifts taken modulo 2.
All inputs are finite; a program needn't handle non-finite values.
Results may differ from the reference program's by a relative error of at most 0.0036.
Values may be sent and summed in bfloat16 or wider, within the bound.
A program may use at most 64 MiB of HBM per device.

```python
import math
import jax
import jax.numpy as jnp
from jax import lax

ORB = 512
HW = 4
NQ = 4
NW = 8
NB = 4
MOMS = 2
SLABS = 4
TILES = 4
ESLAB = 4


def draw_mom_shift(key, part):
    first_key = jax.random.fold_in(key, 11)
    second_key = jax.random.fold_in(key, 23)
    order_key = jax.random.fold_in(key, 37)
    multi_key = jax.random.fold_in(key, 53)
    residues = jax.random.permutation(first_key, MOMS).astype(jnp.int32)
    multiples = jax.random.randint(multi_key, (MOMS,), 0, 4).astype(jnp.int32)
    multiples = jnp.where(residues == 0, 0, jnp.where(residues == MOMS - 1, 3, multiples)).astype(jnp.int32)
    covered = (residues + MOMS * multiples).astype(jnp.int32)
    extra = jax.random.randint(second_key, (NQ - MOMS,), 0, 4 * MOMS).astype(jnp.int32)
    joined = jnp.concatenate([covered, extra])
    return jax.random.permutation(order_key, joined).astype(jnp.int32)


def place_ends(result, own_key, least, largest):
    place = [jax.random.randint(jax.random.fold_in(own_key, axis), (), 0, length) for axis, length in enumerate(result.shape)]
    longest = result.shape.index(max(result.shape))
    beside = place[:longest] + [(place[longest] + 1) % result.shape[longest]] + place[longest + 1:]
    return result.at[tuple(place)].set(least).at[tuple(beside)].set(largest)


def level_of(key, dims, cuts, smallest, high):
    factor_of, own = 1.0, jax.random.fold_in(key, 6)
    for axis_at, parts in cuts:
        draws = jnp.exp(jax.random.uniform(jax.random.fold_in(own, axis_at), (parts,), jnp.float32, smallest / len(cuts), high / len(cuts)))
        factor_of = factor_of * jnp.repeat(draws, dims[axis_at] // parts).reshape([-1 if axis == axis_at else 1 for axis in range(len(dims))])
    return factor_of


def scatter_about(rng, shape, deviation, reach, split=(), held_as=jnp.bfloat16):
    result = deviation * jax.random.normal(rng, shape, jnp.float32)
    if split:
        result = result * level_of(rng, shape, split, -0.22, 0.18)
    return jnp.clip(result, -reach, reach).astype(held_as)


def setup_inputs(seed: int = 0) -> dict:
    key_of = jax.random.split(jax.random.key(seed), 7)
    return {
        "green_ret": scatter_about(key_of[0], (MOMS, SLABS, ESLAB, ORB, 2 * ORB), ORB ** -0.5, 0.25, ((0, 2), (1, 4), (2, 4))),
        "injection": jnp.clip(jnp.exp(math.log(1.0) - 2.3025851 * jax.random.uniform(key_of[1], (MOMS, SLABS, ESLAB, ORB), jnp.float32) ** level_of(key_of[1], (MOMS, SLABS, ESLAB, ORB), ((0, 2), (1, 4), (2, 4)), -0.2, 0.2)), 0.1, 1.0),
        "mom_shift": draw_mom_shift(jax.random.fold_in(key_of[6], 71), 0),
        "phon_off": place_ends(jax.random.randint(key_of[3], (NW,), 0 - HW, HW + 1), jax.random.fold_in(key_of[3], 1), 0 - HW, HW).astype(jnp.int32),
        "coupling": jnp.clip(jnp.exp(jax.random.uniform(key_of[4], (NQ, NW), jnp.float32, math.log(0.05), math.log(1.0))), 0.05, 1.0),
        "tile_nbr": place_ends(jax.random.randint(key_of[5], (TILES, NB), 0, TILES), jax.random.fold_in(key_of[5], 1), 0, TILES - 1).astype(jnp.int32),
    }


def lesser_point(item):
    block, gamma = item
    re = block[:, :ORB].astype(jnp.float32)
    im = block[:, ORB:].astype(jnp.float32)
    left_re = jnp.concatenate([re * gamma[None, :], im * gamma[None, :]], axis=1).astype(jnp.bfloat16)
    left_im = jnp.concatenate([im * gamma[None, :], -re * gamma[None, :]], axis=1).astype(jnp.bfloat16)
    real = jnp.dot(left_re, block.T, preferred_element_type=jnp.float32)
    imag = jnp.dot(left_im, block.T, preferred_element_type=jnp.float32)
    return jnp.concatenate([real, imag], axis=1).astype(jnp.bfloat16)


def reference(green_ret, injection, mom_shift, phon_off, coupling, tile_nbr):
    moms = green_ret.shape[0]
    energies = green_ret.shape[1] * green_ret.shape[2]
    flat = green_ret.reshape(moms * energies, ORB, 2 * ORB)
    gam = injection.reshape(moms * energies, ORB)
    lesser = lax.map(lesser_point, (flat, gam)).reshape(moms, energies, ORB, 2 * ORB)
    padded = jnp.pad(lesser, ((0, 0), (HW, HW), (0, 0), (0, 0)))
    rows = ORB // TILES
    coltile = jnp.arange(ORB, dtype=jnp.int32) // rows
    colmask = jnp.any(coltile[None, :, None] == tile_nbr[:, None, :], axis=2).astype(jnp.float32)
    full_mask = colmask[coltile]
    full_mask = jnp.concatenate([full_mask, full_mask], axis=1)

    def one_momentum(k):
        acc = jnp.zeros((energies, ORB, 2 * ORB), jnp.float32)
        for s in range(NQ):
            src = jnp.mod(k - mom_shift[s], moms).astype(jnp.int32)
            for o in range(NW):
                start = (HW + phon_off[o]).astype(jnp.int32)
                piece = lax.dynamic_slice(padded, (src, start, jnp.int32(0), jnp.int32(0)), (1, energies, ORB, 2 * ORB))[0]
                acc = acc + coupling[s, o] * piece.astype(jnp.float32)
        return (acc * full_mask[None]).astype(jnp.bfloat16)

    out = lax.map(one_momentum, jnp.arange(moms, dtype=jnp.int32))
    return out.reshape(green_ret.shape)
```

```python
import jax
import jax.numpy as jnp
from jax import lax
from jax.experimental import pallas as pl
from jax.experimental.pallas import tpu as pltpu
from jax.sharding import PartitionSpec as P

HW = 4
NW = 8
LANES = 128
PACK = 16
MESH = pl.DeviceIdType.MESH


def fused_kernel(
    nt, nm, nz, g_ref, gam_ref, shift_ref, off_ref, coup_ref, nbr_ref, out_ref,
    left, stage, held, fin, parts, tab,
    a_send, a_recv, z_send, z_recv, near_send, near_recv, far_send, far_recv, own_sem,
):
    t, m, z = lax.axis_index("tile"), lax.axis_index("mom"), lax.axis_index("ewin")
    orb, width = g_ref.shape
    tall = orb // nt
    qr = tall // nm // 2
    hq = qr // 2
    has_up, has_down = z < nz - 1, z > 0

    def dev(tt, mm, zz):
        return {"tile": tt, "mom": mm, "ewin": zz}

    def order(q):
        return q + (q // 2) * (5 - 2 * q)

    ring = order(t)

    def tile_at(i):
        return order(lax.rem(ring + i, nt))

    def mom_at(j):
        return lax.rem(m + j, nm)

    def share(mm):
        return lax.rem(mm + z, nm)

    mine = share(m)
    up_mom, down_mom = mom_at(nm - 1), mom_at(1 % nm)
    pairs = [(i, j) for i in range(nt) for j in range(nm)]
    barrier = pltpu.get_barrier_semaphore()
    for i, j in pairs[1:]:
        pl.semaphore_signal(barrier, inc=1, device_id=dev(tile_at(i), mom_at(j), z), device_id_type=MESH)

    @pl.when(has_up)
    def _():
        pl.semaphore_signal(barrier, inc=1, device_id=dev(t, up_mom, z + 1), device_id_type=MESH)

    @pl.when(has_down)
    def _():
        pl.semaphore_signal(barrier, inc=1, device_id=dev(t, down_mom, z - 1), device_id_type=MESH)

    def tile_rows(tile):
        return pl.ds(pl.multiple_of(tile * tall, tall), tall)

    def times(slot, right):
        both = lax.dot_general(
            left[slot], right, (((1,), (1,)), ((), ())), preferred_element_type=jnp.float32
        )
        return both[:tall], both[tall:]

    def scale_rows(i):
        rows = g_ref[tile_rows(tile_at(i)), :]
        re = rows[:, :orb].astype(jnp.float32) * gam_ref[...]
        im = rows[:, orb:].astype(jnp.float32) * gam_ref[...]
        left[i, :tall, :orb] = re.astype(jnp.bfloat16)
        left[i, :tall, orb:] = im.astype(jnp.bfloat16)
        left[i, tall:, :orb] = im.astype(jnp.bfloat16)
        left[i, tall:, orb:] = (-re).astype(jnp.bfloat16)

    def triangle():
        return (lax.broadcasted_iota(jnp.int32, (tall, tall), d) for d in (0, 1))

    def put_cross(a):
        first, second = lax.rem(a - ring + nt, nt), lax.rem(a + 2 - ring + nt, nt)
        re, im = times(first, g_ref[tile_rows(order(a + 2)), :])
        re = re.reshape(2, nm, qr, tall).astype(jnp.bfloat16)
        im = im.reshape(2, nm, qr, tall).astype(jnp.bfloat16)
        for h, i in enumerate((first, second)):
            stage[i, :, 0, :, :tall] = re[h]
            stage[i, :, 0, :, tall:] = im[h]

    def put_pair(i):
        here, there = g_ref[tile_rows(tile_at(i)), :], g_ref[tile_rows(tile_at(i + 1)), :]
        re, im = times(i, jnp.concatenate([here, there], axis=0))
        row, col = triangle()
        both = jnp.where(row > col, im[:, :tall], re[:, :tall]).reshape(nm, 2, qr, tall).astype(jnp.bfloat16)
        stage[i, :, 3, :, :tall] = both[:, 0]
        stage[i, :, 3, :, tall:] = both[:, 1]
        for cols, block in ((slice(0, tall), re[:, tall:]), (slice(tall, 2 * tall), im[:, tall:])):
            block = block.reshape(2, nm, 2, hq, tall).astype(jnp.bfloat16)
            for h in range(2):
                for b in range(2):
                    stage[(i + h) % nt, :, 1 + b, h * hq : (h + 1) * hq, cols] = block[h, :, b]

    groups = ((0, 1), (1, 1), (2, 2))
    slots = (0, 1, 3, 2)

    def slot_of(i, j):
        return slots[i] * nm + j

    def a_copy(g, i, j):
        v, n = groups[g]
        to = mom_at(j)
        return pltpu.make_async_remote_copy(
            src_ref=stage.at[i, share(to), pl.ds(v, n)],
            dst_ref=held.at[1, pl.ds(v, n), slot_of(i, j)],
            send_sem=a_send.at[g, i, j],
            recv_sem=a_recv.at[g, i, j],
            device_id=dev(tile_at(i), to, z),
            device_id_type=MESH,
        )

    def own_copy():
        return pltpu.make_async_copy(stage.at[0, mine], held.at[1, pl.ds(0, 4), 0], own_sem)

    def send(g, i):
        for j in range(nm):
            if (i, j) != (0, 0):
                a_copy(g, i, j).start()

    def arrived(g, i):
        for j in range(nm):
            if (i, j) != (0, 0):
                a_copy(g, i, j).wait_recv()

    chunks = (
        (0, 1, 0, 1), (1, 3, 0, 1), (0, 4, 1, nm - 1),
        (0, 1, nm, 2 * nm), (0, 1, 3 * nm, nm),
        (1, 1, nm, 3 * nm), (2, 1, nm, 3 * nm), (3, 1, nm, 3 * nm),
    )
    needs = ((0, 2, 3, 4), (1, 5), (6,), (7,))

    def z_copy(k, up):
        v, n, s, w = chunks[k]
        side = 0 if up else 1
        if s == 0:
            src, dst = stage.at[0, mine, pl.ds(v, n)], held.at[2 * side, pl.ds(v, n), 0]
        else:
            src, dst = held.at[1, pl.ds(v, n), pl.ds(s, w)], held.at[2 * side, pl.ds(v, n), pl.ds(s, w)]
        return pltpu.make_async_remote_copy(
            src_ref=src,
            dst_ref=dst,
            send_sem=z_send.at[side, k],
            recv_sem=z_recv.at[side, k],
            device_id=dev(t, up_mom if up else down_mom, z + 1 if up else z - 1),
            device_id_type=MESH,
        )

    def pass_on(k):
        @pl.when(has_up)
        def _():
            z_copy(k, True).start()

        @pl.when(has_down)
        def _():
            z_copy(k, False).start()

    for i in range(nt):
        scale_rows(i)
    near_a = lax.rem(ring, 2)
    put_cross(near_a)
    pl.semaphore_wait(barrier, nt * nm - 1 + has_up.astype(jnp.int32) + has_down.astype(jnp.int32))
    send(0, 2)
    send(0, 0)
    pass_on(0)
    put_cross(1 - near_a)
    send(0, 1)
    send(0, 3)
    put_pair(0)
    put_pair(3)
    send(1, 0)
    send(2, 0)
    pass_on(1)
    own_copy().start()
    put_pair(1)
    send(1, 1)
    put_pair(2)
    for g, i in ((1, 3), (1, 2), (2, 1), (2, 3), (2, 2)):
        send(g, i)
    for g in range(3):
        arrived(g, 0)
    pass_on(2)

    @pl.when(jnp.logical_not(has_down))
    def _():
        held[0] = jnp.zeros(held.shape[1:], held.dtype)

    @pl.when(jnp.logical_not(has_up))
    def _():
        held[2] = jnp.zeros(held.shape[1:], held.dtype)

    shifts = [lax.rem(lax.rem(shift_ref[s], nm) + nm, nm) for s in range(shift_ref.shape[0])]
    for diff in range(nm):
        per_off = []
        for o in range(NW):
            acc = jnp.float32(0.0)
            for s in range(len(shifts)):
                acc = acc + jnp.where(shifts[s] == diff, coup_ref[s, o], 0.0)
            per_off.append(acc)
        for d in range(2 * HW + 1):
            acc = jnp.float32(0.0)
            for o in range(NW):
                acc = acc + jnp.where(off_ref[o] + HW == d, per_off[o], 0.0)
            tab[diff, d] = acc

    for i in (1, 3):
        arrived(0, i)
    pass_on(3)
    arrived(0, 2)
    pass_on(4)
    for i in (1, 3, 2):
        arrived(1, i)
    pass_on(5)
    for i in (1, 3, 2):
        arrived(2, i)
    pass_on(6)
    pass_on(7)
    own_copy().wait()

    bases = []
    for p in range(nt):
        i = lax.rem(ring - order(p) + nt, nt)
        bases.append((i + (i // 2) * (5 - 2 * i)) * nm)

    def block_lo(block, who):
        return pl.multiple_of((block * nm + share(who)) * qr, qr)

    def pieces(v, who, here):
        if v == 0:
            block = ring // 2 if here else 1 - ring // 2
            return [(0, qr, 2, block_lo(block, who), 2, 2)]
        if v == 3:
            return [(3 * qr, qr, 3, block_lo(0, who), None, None)]
        off = (v - 1) * hq
        return [
            (v * qr + h * hq, hq, h, pl.multiple_of(block_lo(h, who) + off, hq), 1 - h, 1 if h == 0 else nt - 1)
            for h in range(2)
        ]

    def near_copy(v, h, kk, who):
        lo, n, slot, row, _, _ = pieces(v, who, True)[h]
        return pltpu.make_async_remote_copy(
            src_ref=fin.at[kk, :, pl.ds(lo, n)],
            dst_ref=parts.at[slot, :, pl.ds(row, n)],
            send_sem=near_send.at[v, h, kk],
            recv_sem=near_recv.at[v, h, kk],
            device_id=dev(t, mom_at(kk), z),
            device_id_type=MESH,
        )

    def far_copy(v, h, kk, who, here):
        lo, n, _, row, slot, step = pieces(v, who, here)[h]
        return pltpu.make_async_remote_copy(
            src_ref=fin.at[kk, :, pl.ds(lo, n)],
            dst_ref=parts.at[slot, :, pl.ds(row, n)],
            send_sem=far_send.at[v, h, kk],
            recv_sem=far_recv.at[v, h, kk],
            device_id=dev(tile_at(step), mom_at(kk), z),
            device_id_type=MESH,
        )

    def halves(v):
        return range(2 if v in (1, 2) else 1)

    def mix(v):
        for k in needs[v]:
            @pl.when(has_down)
            def _():
                z_copy(k, True).wait_recv()

            @pl.when(has_up)
            def _():
                z_copy(k, False).wait_recv()

        own = pieces(v, m, True)
        weight = [[tab[diff, d] for d in range(2 * HW + 1)] for diff in range(nm)]
        wide = 2 * tall // LANES
        for lo, n, slot, row, _, _ in own:
            @pl.loop(0, n // PACK * wide)
            def _(step):
                r = pl.multiple_of((step // wide) * PACK, PACK)
                inner = pl.ds(pl.multiple_of(lo - v * qr + r, PACK), PACK)
                rows = pl.ds(pl.multiple_of(lo + r, PACK), PACK)
                cols = pl.ds(pl.multiple_of((step % wide) * LANES, LANES), LANES)
                acc = [[None] * nt for _ in range(nm)]
                for zs in range(3):
                    for p in range(nt):
                        src = zs * nt + p
                        for j in range(nm):
                            x = held[zs, v, bases[p] + j, inner, cols].astype(jnp.float32)
                            for kk in range(nm):
                                for e in range(nt):
                                    if 0 <= src - e <= 2 * HW:
                                        term = weight[(kk + j + zs - 1) % nm][src - e] * x
                                        acc[kk][e] = term if acc[kk][e] is None else acc[kk][e] + term
                for e in range(nt):
                    for kk in range(nm):
                        value = acc[kk][e].astype(jnp.bfloat16)
                        if kk == 0:
                            parts[slot, e, pl.ds(pl.multiple_of(row + r, PACK), PACK), cols] = value
                        if kk > 0 or v < 3:
                            fin[kk, e, rows, cols] = value

        for h in halves(v):
            for kk in range(nm):
                if v < 3:
                    far_copy(v, h, kk, m, True).start()
                if kk > 0:
                    near_copy(v, h, kk, m).start()

    def landed(v):
        for h in halves(v):
            for kk in range(nm):
                who = mom_at(nm - kk)
                if v < 3:
                    far_copy(v, h, kk, who, False).wait_recv()
                if kk > 0:
                    near_copy(v, h, kk, who).wait_recv()

    def kept(tile):
        found = jnp.float32(0.0)
        for b in range(nbr_ref.shape[1]):
            found = jnp.where(nbr_ref[t, b] == tile, 1.0, found)
        return found

    def store(part, tile, flip):
        keep = kept(tile)

        @pl.loop(0, nt)
        def _(e):
            re, im = parts[part, e, :, :tall].astype(jnp.float32), parts[part, e, :, tall:].astype(jnp.float32)
            if flip:
                re, im = re.T, -im.T
            re, im = (re * keep).astype(jnp.bfloat16), (im * keep).astype(jnp.bfloat16)
            out_ref[e, :, pl.ds(pl.multiple_of(tile * tall, tall), tall)] = re
            out_ref[e, :, pl.ds(pl.multiple_of(orb + tile * tall, tall), tall)] = im

    def store_diagonal():
        row, col = triangle()
        keep = kept(t)

        @pl.loop(0, nt)
        def _(e):
            packed = [
                parts[3, e, c * qr : (c + 1) * qr, h * tall : (h + 1) * tall] for c in range(nm) for h in range(2)
            ]
            both = jnp.concatenate(packed, axis=0).astype(jnp.float32)
            turned = both.T
            re = jnp.where(row > col, turned, both)
            im = jnp.where(row > col, both, jnp.where(row < col, -turned, 0.0))
            out_ref[e, :, pl.ds(pl.multiple_of(t * tall, tall), tall)] = (re * keep).astype(jnp.bfloat16)
            out_ref[e, :, pl.ds(pl.multiple_of(orb + t * tall, tall), tall)] = (im * keep).astype(jnp.bfloat16)

    for v in range(3):
        mix(v)
    landed(0)

    @pl.when(ring < 2)
    def _():
        store(2, tile_at(2), False)

    @pl.when(ring >= 2)
    def _():
        store(2, tile_at(2), True)

    mix(3)
    landed(1)
    landed(2)
    store(0, tile_at(1), False)
    store(1, tile_at(nt - 1), True)
    landed(3)
    store_diagonal()

    for v in range(4):
        for h in halves(v):
            for kk in range(nm):
                if v < 3:
                    far_copy(v, h, kk, m, True).wait_send()
                if kk > 0:
                    near_copy(v, h, kk, m).wait_send()
    for i, j in pairs[1:]:
        for g in range(3):
            a_copy(g, i, j).wait_send()
    for k in range(len(chunks)):
        @pl.when(has_up)
        def _():
            z_copy(k, True).wait_send()

        @pl.when(has_down)
        def _():
            z_copy(k, False).wait_send()


def fused(green_ret, injection, mom_shift, phon_off, coupling, tile_nbr):
    nt, nm, nz = lax.axis_size("tile"), lax.axis_size("mom"), lax.axis_size("ewin")
    orbitals, width = green_ret.shape[3:]
    tall = orbitals // nt
    qr = tall // nm // 2
    green = green_ret.reshape(orbitals, width)
    gamma = injection.reshape(1, orbitals)
    vmem, smem = pl.BlockSpec(memory_space=pltpu.VMEM), pl.BlockSpec(memory_space=pltpu.SMEM)
    dma = pltpu.SemaphoreType.DMA
    total = pl.pallas_call(
        lambda *refs: fused_kernel(nt, nm, nz, *refs),
        out_shape=pltpu.VMEM((nt, tall, width), jnp.bfloat16),
        in_specs=[vmem, vmem, smem, smem, smem, smem],
        out_specs=vmem,
        scratch_shapes=[
            pltpu.VMEM((nt, 2 * tall, width), jnp.bfloat16),
            pltpu.VMEM((nt, nm, 4, qr, 2 * tall), jnp.bfloat16),
            pltpu.VMEM((3, 4, nt * nm, qr, 2 * tall), jnp.bfloat16),
            pltpu.VMEM((nm, nt, 4 * qr, 2 * tall), jnp.bfloat16),
            pltpu.VMEM((4, nt, tall, 2 * tall), jnp.bfloat16),
            pltpu.SMEM((nm, 2 * HW + 1), jnp.float32),
            dma((3, nt, nm)),
            dma((3, nt, nm)),
            dma((2, 8)),
            dma((2, 8)),
            dma((4, 2, nm)),
            dma((4, 2, nm)),
            dma((4, 2, nm)),
            dma((4, 2, nm)),
            dma,
        ],
        compiler_params=pltpu.CompilerParams(collective_id=0, has_side_effects=True),
    )(green, gamma, mom_shift, phon_off, coupling, tile_nbr)
    return total[None, None]


def with_halo(shard, sides, width):
    for axis, dim in sides:
        peers, length = (lax.axis_size(axis), shard.shape[dim])
        up = [(i, (i + 1) % peers) for i in range(peers - 1)]
        down = [(j, i) for i, j in up]
        last = lax.slice_in_dim(shard, length - width, length, axis=dim)
        initial = lax.slice_in_dim(shard, 0, width, axis=dim)
        before = lax.ppermute(last, axis, up)
        after = lax.ppermute(initial, axis, down)
        shard = jnp.concatenate([before, shard, after], axis=dim)
    return shard


def on_device(green_ret, injection, mom_shift, phon_off, coupling, tile_nbr):
    blocks = green_ret[0, 0]
    gamma = injection[0, 0]
    orbitals = blocks.shape[1]
    ntiles = lax.axis_size("tile")
    per_tile = orbitals // ntiles
    real_part = blocks[:, :, :orbitals].astype(jnp.float32)
    imag_part = blocks[:, :, orbitals:].astype(jnp.float32)
    scale = gamma[:, None, :]
    left_re = jnp.concatenate([real_part * scale, imag_part * scale], axis=2).astype(jnp.bfloat16)
    left_im = jnp.concatenate([imag_part * scale, -real_part * scale], axis=2).astype(jnp.bfloat16)
    real_out = jnp.einsum("prk,pck->prc", left_re, blocks, preferred_element_type=jnp.float32)
    imag_out = jnp.einsum("prk,pck->prc", left_im, blocks, preferred_element_type=jnp.float32)
    payload = jnp.concatenate([real_out, imag_out], axis=2).astype(jnp.bfloat16)
    exchanged = lax.all_to_all(payload, "tile", split_axis=1, concat_axis=0, tiled=True)
    energies = exchanged.shape[0]
    rimmed = with_halo(exchanged, (("ewin", 0),), HW)
    extended = lax.all_gather(rimmed[None], "mom", axis=0, tiled=True)
    nmom = lax.axis_size("mom")
    here = lax.axis_index("mom")
    source = jnp.mod(here - mom_shift, nmom)
    onehot = (source[:, None] == jnp.arange(nmom, dtype=jnp.int32)[None, :]).astype(jnp.float32)
    weights = jnp.dot(onehot.T, coupling, precision=lax.Precision.HIGHEST)
    total = jnp.zeros(exchanged.shape, jnp.float32)
    for offset in range(NW):
        start = HW + phon_off[offset]
        piece = lax.dynamic_slice_in_dim(extended, start, energies, 1)
        for moment in range(nmom):
            total = total + weights[moment, offset] * piece[moment].astype(jnp.float32)
    tile_here = lax.axis_index("tile")
    neighbours = lax.dynamic_index_in_dim(tile_nbr, tile_here, 0, keepdims=False)
    coltile = jnp.arange(orbitals, dtype=jnp.int32) // per_tile
    colmask = jnp.any(coltile[:, None] == neighbours[None, :], axis=1).astype(jnp.float32)
    colmask = jnp.concatenate([colmask, colmask])
    result = (total * colmask[None, None, :]).astype(jnp.bfloat16)
    return result[None, None]


def body_for(mesh):
    nt, nm = mesh.shape["tile"], mesh.shape["mom"]

    def body(green_ret, *rest):
        points, orbitals = green_ret.shape[2:4]
        aligned = orbitals % (nt * LANES) == 0 and orbitals % (nt * nm * 4 * PACK) == 0
        if aligned and points == 1 and nt == HW:
            return fused(green_ret, *rest)
        return on_device(green_ret, *rest)

    return body


def solution(mesh):
    placed = (
        P("mom", "ewin", "tile", None, None),
        P("mom", "ewin", "tile", None),
        P(),
        P(),
        P(),
        P(),
    )
    return jax.shard_map(
        body_for(mesh),
        mesh=mesh,
        in_specs=placed,
        out_specs=P("mom", "ewin", None, "tile", None),
        check_vma=False,
    )
```

```python
import jax
import jax.numpy as jnp
from jax import lax
from jax.experimental import pallas as pl
from jax.experimental.pallas import tpu as pltpu
from jax.sharding import PartitionSpec as P

HW = 4
NW = 8
LANES = 128
PACK = 16
MESH = pl.DeviceIdType.MESH


def fused_kernel(
    nt, nm, nz, g_hbm, gam_hbm, shift_hbm, off_hbm, coup_hbm, nbr_hbm, out_ref,
    g_ref, gam_ref, shift_ref, off_ref, coup_ref, nbr_ref, left, stage, held, fin, parts, tab,
    load_sem, a_send, a_recv, z_send, z_recv, near_send, near_recv, far_send, far_recv, own_sem,
):
    t, m, z = lax.axis_index("tile"), lax.axis_index("mom"), lax.axis_index("ewin")
    orb, width = g_hbm.shape
    tall = orb // nt
    qr = tall // nm // 2
    hq = qr // 2
    has_up, has_down = z < nz - 1, z > 0

    def dev(tt, mm, zz):
        return {"tile": tt, "mom": mm, "ewin": zz}

    def order(q):
        return q + (q // 2) * (5 - 2 * q)

    ring = order(t)

    def tile_at(i):
        return order(lax.rem(ring + i, nt))

    def tile_rows(tile):
        return pl.ds(pl.multiple_of(tile * tall, tall), tall)

    def load(i):
        rows = tile_rows(tile_at(i))
        return pltpu.make_async_copy(g_hbm.at[rows], g_ref.at[rows], load_sem.at[i])

    loads = [pltpu.make_async_copy(gam_hbm, gam_ref, load_sem.at[nt])]
    loads += [load(i) for i in (0, 2, 1, 3)]
    small = ((shift_hbm, shift_ref), (off_hbm, off_ref), (coup_hbm, coup_ref), (nbr_hbm, nbr_ref))
    small = [pltpu.make_async_copy(src, dst, load_sem.at[nt + 1 + n]) for n, (src, dst) in enumerate(small)]
    for copy in loads + small:
        copy.start()

    def mom_at(j):
        return lax.rem(m + j, nm)

    def share(mm):
        return lax.rem(mm + z, nm)

    mine = share(m)
    up_mom, down_mom = mom_at(nm - 1), mom_at(1 % nm)
    pairs = [(i, j) for i in range(nt) for j in range(nm)]
    barrier = pltpu.get_barrier_semaphore()
    for i, j in pairs[1:]:
        pl.semaphore_signal(barrier, inc=1, device_id=dev(tile_at(i), mom_at(j), z), device_id_type=MESH)

    @pl.when(has_up)
    def _():
        pl.semaphore_signal(barrier, inc=1, device_id=dev(t, up_mom, z + 1), device_id_type=MESH)

    @pl.when(has_down)
    def _():
        pl.semaphore_signal(barrier, inc=1, device_id=dev(t, down_mom, z - 1), device_id_type=MESH)

    def times(slot, right):
        both = lax.dot_general(
            left[slot], right, (((1,), (1,)), ((), ())), preferred_element_type=jnp.float32
        )
        return both[:tall], both[tall:]

    def scale_rows(i):
        rows = g_ref[tile_rows(tile_at(i)), :]
        re = rows[:, :orb].astype(jnp.float32) * gam_ref[...]
        im = rows[:, orb:].astype(jnp.float32) * gam_ref[...]
        left[i, :tall, :orb] = re.astype(jnp.bfloat16)
        left[i, :tall, orb:] = im.astype(jnp.bfloat16)
        left[i, tall:, :orb] = im.astype(jnp.bfloat16)
        left[i, tall:, orb:] = (-re).astype(jnp.bfloat16)

    def triangle():
        return (lax.broadcasted_iota(jnp.int32, (tall, tall), d) for d in (0, 1))

    def put_cross(a):
        first, second = lax.rem(a - ring + nt, nt), lax.rem(a + 2 - ring + nt, nt)
        re, im = times(first, g_ref[tile_rows(order(a + 2)), :])
        re = re.reshape(2, nm, qr, tall).astype(jnp.bfloat16)
        im = im.reshape(2, nm, qr, tall).astype(jnp.bfloat16)
        for h, i in enumerate((first, second)):
            stage[i, :, 0, :, :tall] = re[h]
            stage[i, :, 0, :, tall:] = im[h]

    def put_pair(i):
        here, there = g_ref[tile_rows(tile_at(i)), :], g_ref[tile_rows(tile_at(i + 1)), :]
        re, im = times(i, jnp.concatenate([here, there], axis=0))
        row, col = triangle()
        both = jnp.where(row > col, im[:, :tall], re[:, :tall]).reshape(nm, 2, qr, tall).astype(jnp.bfloat16)
        stage[i, :, 3, :, :tall] = both[:, 0]
        stage[i, :, 3, :, tall:] = both[:, 1]
        for cols, block in ((slice(0, tall), re[:, tall:]), (slice(tall, 2 * tall), im[:, tall:])):
            block = block.reshape(2, nm, 2, hq, tall).astype(jnp.bfloat16)
            for h in range(2):
                for b in range(2):
                    stage[(i + h) % nt, :, 1 + b, h * hq : (h + 1) * hq, cols] = block[h, :, b]

    groups = ((0, 1), (1, 1), (2, 2))
    slots = (0, 1, 3, 2)

    def slot_of(i, j):
        return slots[i] * nm + j

    def a_copy(g, i, j):
        v, n = groups[g]
        to = mom_at(j)
        return pltpu.make_async_remote_copy(
            src_ref=stage.at[i, share(to), pl.ds(v, n)],
            dst_ref=held.at[1, pl.ds(v, n), slot_of(i, j)],
            send_sem=a_send.at[g, i, j],
            recv_sem=a_recv.at[g, i, j],
            device_id=dev(tile_at(i), to, z),
            device_id_type=MESH,
        )

    def own_copy():
        return pltpu.make_async_copy(stage.at[0, mine], held.at[1, pl.ds(0, 4), 0], own_sem)

    def send(g, i):
        for j in range(nm):
            if (i, j) != (0, 0):
                a_copy(g, i, j).start()

    def arrived(g, i):
        for j in range(nm):
            if (i, j) != (0, 0):
                a_copy(g, i, j).wait_recv()

    chunks = (
        (0, 1, 0, 1), (1, 3, 0, 1), (0, 1, 1, nm - 1),
        (0, 1, nm, 2 * nm), (0, 1, 3 * nm, nm), (1, 3, 1, nm - 1),
        (1, 1, nm, 3 * nm), (2, 1, nm, 3 * nm), (3, 1, nm, 3 * nm),
    )
    needs = ((0, 2, 3, 4), (1, 5, 6), (7,), (8,))

    def z_copy(k, up):
        v, n, s, w = chunks[k]
        side = 0 if up else 1
        if s == 0:
            src, dst = stage.at[0, mine, pl.ds(v, n)], held.at[2 * side, pl.ds(v, n), 0]
        else:
            src, dst = held.at[1, pl.ds(v, n), pl.ds(s, w)], held.at[2 * side, pl.ds(v, n), pl.ds(s, w)]
        return pltpu.make_async_remote_copy(
            src_ref=src,
            dst_ref=dst,
            send_sem=z_send.at[side, k],
            recv_sem=z_recv.at[side, k],
            device_id=dev(t, up_mom if up else down_mom, z + 1 if up else z - 1),
            device_id_type=MESH,
        )

    def pass_on(k):
        @pl.when(has_up)
        def _():
            z_copy(k, True).start()

        @pl.when(has_down)
        def _():
            z_copy(k, False).start()

    for copy in loads:
        copy.wait()
    for i in range(nt):
        scale_rows(i)
    near_a = lax.rem(ring, 2)
    put_cross(near_a)
    pl.semaphore_wait(barrier, nt * nm - 1 + has_up.astype(jnp.int32) + has_down.astype(jnp.int32))
    send(0, 2)
    send(0, 0)
    pass_on(0)
    put_cross(1 - near_a)
    send(0, 1)
    send(0, 3)
    put_pair(0)
    put_pair(3)
    send(1, 0)
    send(2, 0)
    pass_on(1)
    own_copy().start()
    put_pair(1)
    send(1, 1)
    put_pair(2)
    for g, i in ((1, 3), (1, 2), (2, 1), (2, 3), (2, 2)):
        send(g, i)
    arrived(0, 0)
    pass_on(2)
    for i in (1, 3):
        arrived(0, i)
    pass_on(3)
    arrived(0, 2)
    pass_on(4)
    for g in (1, 2):
        arrived(g, 0)
    pass_on(5)

    @pl.when(jnp.logical_not(has_down))
    def _():
        held[0] = jnp.zeros(held.shape[1:], held.dtype)

    @pl.when(jnp.logical_not(has_up))
    def _():
        held[2] = jnp.zeros(held.shape[1:], held.dtype)

    for copy in small:
        copy.wait()
    shifts = [lax.rem(lax.rem(shift_ref[s], nm) + nm, nm) for s in range(shift_ref.shape[0])]
    table = []
    for diff in range(nm):
        per_off = []
        for o in range(NW):
            acc = jnp.float32(0.0)
            for s in range(len(shifts)):
                acc = acc + jnp.where(shifts[s] == diff, coup_ref[s, o], 0.0)
            per_off.append(acc)
        row = []
        for d in range(2 * HW + 1):
            acc = jnp.float32(0.0)
            for o in range(NW):
                acc = acc + jnp.where(off_ref[o] + HW == d, per_off[o], 0.0)
            row.append(acc)
        table.append(row)
    for d in range(2 * HW + 1):
        tab[0, d] = 0.5 * (table[0][d] + table[1][d])
        tab[1, d] = 0.5 * (table[0][d] - table[1][d])

    for i in (1, 3, 2):
        arrived(1, i)
    pass_on(6)
    own_copy().wait()

    bases = []
    for p in range(nt):
        i = lax.rem(ring - order(p) + nt, nt)
        bases.append((i + (i // 2) * (5 - 2 * i)) * nm)

    def block_lo(block, who):
        return pl.multiple_of((block * nm + share(who)) * qr, qr)

    def pieces(v, who, here):
        if v == 0:
            block = ring // 2 if here else 1 - ring // 2
            return [(0, qr, 2, block_lo(block, who), 2, 2)]
        if v == 3:
            return [(3 * qr, qr, 3, block_lo(0, who), None, None)]
        off = (v - 1) * hq
        return [
            (v * qr + h * hq, hq, h, pl.multiple_of(block_lo(h, who) + off, hq), 1 - h, 1 if h == 0 else nt - 1)
            for h in range(2)
        ]

    def near_copy(v, h, kk, who):
        lo, n, slot, row, _, _ = pieces(v, who, True)[h]
        return pltpu.make_async_remote_copy(
            src_ref=fin.at[kk, :, pl.ds(lo, n)],
            dst_ref=parts.at[slot, :, pl.ds(row, n)],
            send_sem=near_send.at[v, h, kk],
            recv_sem=near_recv.at[v, h, kk],
            device_id=dev(t, mom_at(kk), z),
            device_id_type=MESH,
        )

    def far_copy(v, h, kk, who, here):
        lo, n, _, row, slot, step = pieces(v, who, here)[h]
        return pltpu.make_async_remote_copy(
            src_ref=fin.at[kk, :, pl.ds(lo, n)],
            dst_ref=parts.at[slot, :, pl.ds(row, n)],
            send_sem=far_send.at[v, h, kk],
            recv_sem=far_recv.at[v, h, kk],
            device_id=dev(tile_at(step), mom_at(kk), z),
            device_id_type=MESH,
        )

    def halves(v):
        return range(2 if v in (1, 2) else 1)

    def mix(v):
        for k in needs[v]:
            @pl.when(has_down)
            def _():
                z_copy(k, True).wait_recv()

            @pl.when(has_up)
            def _():
                z_copy(k, False).wait_recv()

        own = pieces(v, m, True)
        weight = [[tab[part, d] for d in range(2 * HW + 1)] for part in range(2)]
        wide = 2 * tall // LANES
        for lo, n, slot, row, _, _ in own:
            for step in range(n // PACK * wide):
                r = step // wide * PACK
                inner = pl.ds(lo - v * qr + r, PACK)
                rows = pl.ds(lo + r, PACK)
                cols = pl.ds(step % wide * LANES, LANES)
                acc = [[None] * nt for _ in range(2)]
                for zs in range(3):
                    for p in range(nt):
                        src = zs * nt + p
                        x = [held[zs, v, bases[p] + (j + zs + 1) % 2, inner, cols].astype(jnp.float32) for j in range(2)]
                        for part, y in enumerate((x[0] + x[1], x[0] - x[1])):
                            for e in range(nt):
                                if 0 <= src - e <= 2 * HW:
                                    term = weight[part][src - e] * y
                                    acc[part][e] = term if acc[part][e] is None else acc[part][e] + term
                for e in range(nt):
                    for kk, value in enumerate((acc[0][e] + acc[1][e], acc[0][e] - acc[1][e])):
                        value = value.astype(jnp.bfloat16)
                        if kk == 0:
                            parts[slot, e, pl.ds(pl.multiple_of(row + r, PACK), PACK), cols] = value
                        if kk > 0 or v < 3:
                            fin[kk, e, rows, cols] = value

        for h in halves(v):
            for kk in range(nm):
                if v < 3:
                    far_copy(v, h, kk, m, True).start()
                if kk > 0:
                    near_copy(v, h, kk, m).start()

    def landed(v):
        for h in halves(v):
            for kk in range(nm):
                who = mom_at(nm - kk)
                if v < 3:
                    far_copy(v, h, kk, who, False).wait_recv()
                if kk > 0:
                    near_copy(v, h, kk, who).wait_recv()

    def kept(tile):
        found = jnp.float32(0.0)
        for b in range(nbr_ref.shape[1]):
            found = jnp.where(nbr_ref[t, b] == tile, 1.0, found)
        return found

    def store(part, tile, flip):
        keep = kept(tile)

        for e in range(nt):
            re, im = parts[part, e, :, :tall].astype(jnp.float32), parts[part, e, :, tall:].astype(jnp.float32)
            if flip:
                re, im = re.T, -im.T
            re, im = (re * keep).astype(jnp.bfloat16), (im * keep).astype(jnp.bfloat16)
            out_ref[e, :, pl.ds(pl.multiple_of(tile * tall, tall), tall)] = re
            out_ref[e, :, pl.ds(pl.multiple_of(orb + tile * tall, tall), tall)] = im

    def store_diagonal():
        row, col = triangle()
        keep = kept(t)

        for e in range(nt):
            packed = [
                parts[3, e, c * qr : (c + 1) * qr, h * tall : (h + 1) * tall] for c in range(nm) for h in range(2)
            ]
            both = jnp.concatenate(packed, axis=0).astype(jnp.float32)
            turned = both.T
            re = jnp.where(row > col, turned, both)
            im = jnp.where(row > col, both, jnp.where(row < col, -turned, 0.0))
            out_ref[e, :, pl.ds(pl.multiple_of(t * tall, tall), tall)] = (re * keep).astype(jnp.bfloat16)
            out_ref[e, :, pl.ds(pl.multiple_of(orb + t * tall, tall), tall)] = (im * keep).astype(jnp.bfloat16)

    mix(0)
    for i in (1, 3, 2):
        arrived(2, i)
    pass_on(7)
    pass_on(8)
    mix(1)
    mix(2)
    landed(0)

    @pl.when(ring < 2)
    def _():
        store(2, tile_at(2), False)

    @pl.when(ring >= 2)
    def _():
        store(2, tile_at(2), True)

    mix(3)
    landed(1)
    landed(2)
    store(0, tile_at(1), False)
    store(1, tile_at(nt - 1), True)
    landed(3)
    store_diagonal()

    for v in range(4):
        for h in halves(v):
            for kk in range(nm):
                if v < 3:
                    far_copy(v, h, kk, m, True).wait_send()
                if kk > 0:
                    near_copy(v, h, kk, m).wait_send()
    for i, j in pairs[1:]:
        for g in range(3):
            a_copy(g, i, j).wait_send()
    for k in range(len(chunks)):
        @pl.when(has_up)
        def _():
            z_copy(k, True).wait_send()

        @pl.when(has_down)
        def _():
            z_copy(k, False).wait_send()


def fused(green_ret, injection, mom_shift, phon_off, coupling, tile_nbr):
    nt, nm, nz = lax.axis_size("tile"), lax.axis_size("mom"), lax.axis_size("ewin")
    orbitals, width = green_ret.shape[3:]
    tall = orbitals // nt
    qr = tall // nm // 2
    green = green_ret.reshape(orbitals, width)
    gamma = injection.reshape(1, orbitals)
    vmem, anywhere = pl.BlockSpec(memory_space=pltpu.VMEM), pl.BlockSpec(memory_space=pl.ANY)
    args = (green, gamma, mom_shift, phon_off, coupling, tile_nbr)
    dma = pltpu.SemaphoreType.DMA
    total = pl.pallas_call(
        lambda *refs: fused_kernel(nt, nm, nz, *refs),
        out_shape=pltpu.VMEM((nt, tall, width), jnp.bfloat16),
        in_specs=[anywhere] * len(args),
        out_specs=vmem,
        scratch_shapes=[
            pltpu.VMEM(green.shape, green.dtype),
            pltpu.VMEM(gamma.shape, gamma.dtype),
            *[pltpu.SMEM(a.shape, a.dtype) for a in args[2:]],
            pltpu.VMEM((nt, 2 * tall, width), jnp.bfloat16),
            pltpu.VMEM((nt, nm, 4, qr, 2 * tall), jnp.bfloat16),
            pltpu.VMEM((3, 4, nt * nm, qr, 2 * tall), jnp.bfloat16),
            pltpu.VMEM((nm, nt, 4 * qr, 2 * tall), jnp.bfloat16),
            pltpu.VMEM((4, nt, tall, 2 * tall), jnp.bfloat16),
            pltpu.SMEM((nm, 2 * HW + 1), jnp.float32),
            dma((nt + 5,)),
            dma((3, nt, nm)),
            dma((3, nt, nm)),
            dma((2, 9)),
            dma((2, 9)),
            dma((4, 2, nm)),
            dma((4, 2, nm)),
            dma((4, 2, nm)),
            dma((4, 2, nm)),
            dma,
        ],
        compiler_params=pltpu.CompilerParams(collective_id=0, has_side_effects=True),
    )(*args)
    return total[None, None]


def with_halo(shard, sides, width):
    for axis, dim in sides:
        peers, length = (lax.axis_size(axis), shard.shape[dim])
        up = [(i, (i + 1) % peers) for i in range(peers - 1)]
        down = [(j, i) for i, j in up]
        last = lax.slice_in_dim(shard, length - width, length, axis=dim)
        initial = lax.slice_in_dim(shard, 0, width, axis=dim)
        before = lax.ppermute(last, axis, up)
        after = lax.ppermute(initial, axis, down)
        shard = jnp.concatenate([before, shard, after], axis=dim)
    return shard


def on_device(green_ret, injection, mom_shift, phon_off, coupling, tile_nbr):
    blocks = green_ret[0, 0]
    gamma = injection[0, 0]
    orbitals = blocks.shape[1]
    ntiles = lax.axis_size("tile")
    per_tile = orbitals // ntiles
    real_part = blocks[:, :, :orbitals].astype(jnp.float32)
    imag_part = blocks[:, :, orbitals:].astype(jnp.float32)
    scale = gamma[:, None, :]
    left_re = jnp.concatenate([real_part * scale, imag_part * scale], axis=2).astype(jnp.bfloat16)
    left_im = jnp.concatenate([imag_part * scale, -real_part * scale], axis=2).astype(jnp.bfloat16)
    real_out = jnp.einsum("prk,pck->prc", left_re, blocks, preferred_element_type=jnp.float32)
    imag_out = jnp.einsum("prk,pck->prc", left_im, blocks, preferred_element_type=jnp.float32)
    payload = jnp.concatenate([real_out, imag_out], axis=2).astype(jnp.bfloat16)
    exchanged = lax.all_to_all(payload, "tile", split_axis=1, concat_axis=0, tiled=True)
    energies = exchanged.shape[0]
    rimmed = with_halo(exchanged, (("ewin", 0),), HW)
    extended = lax.all_gather(rimmed[None], "mom", axis=0, tiled=True)
    nmom = lax.axis_size("mom")
    here = lax.axis_index("mom")
    source = jnp.mod(here - mom_shift, nmom)
    onehot = (source[:, None] == jnp.arange(nmom, dtype=jnp.int32)[None, :]).astype(jnp.float32)
    weights = jnp.dot(onehot.T, coupling, precision=lax.Precision.HIGHEST)
    total = jnp.zeros(exchanged.shape, jnp.float32)
    for offset in range(NW):
        start = HW + phon_off[offset]
        piece = lax.dynamic_slice_in_dim(extended, start, energies, 1)
        for moment in range(nmom):
            total = total + weights[moment, offset] * piece[moment].astype(jnp.float32)
    tile_here = lax.axis_index("tile")
    neighbours = lax.dynamic_index_in_dim(tile_nbr, tile_here, 0, keepdims=False)
    coltile = jnp.arange(orbitals, dtype=jnp.int32) // per_tile
    colmask = jnp.any(coltile[:, None] == neighbours[None, :], axis=1).astype(jnp.float32)
    colmask = jnp.concatenate([colmask, colmask])
    result = (total * colmask[None, None, :]).astype(jnp.bfloat16)
    return result[None, None]


def body_for(mesh):
    nt, nm = mesh.shape["tile"], mesh.shape["mom"]

    def body(green_ret, *rest):
        points, orbitals = green_ret.shape[2:4]
        aligned = orbitals % (nt * LANES) == 0 and orbitals % (nt * nm * 4 * PACK) == 0
        if aligned and points == 1 and nt == HW and nm == 2:
            return fused(green_ret, *rest)
        return on_device(green_ret, *rest)

    return body


def solution(mesh):
    placed = (
        P("mom", "ewin", "tile", None, None),
        P("mom", "ewin", "tile", None),
        P(),
        P(),
        P(),
        P(),
    )
    return jax.shard_map(
        body_for(mesh),
        mesh=mesh,
        in_specs=placed,
        out_specs=P("mom", "ewin", None, "tile", None),
        check_vma=False,
    )
```

```python
import jax
import jax.numpy as jnp
from jax import lax
from jax.experimental import pallas as pl
from jax.experimental.pallas import tpu as pltpu
from jax.sharding import PartitionSpec as P

HW = 4
NW = 8
LANES = 128
PACK = 16
MESH = pl.DeviceIdType.MESH


def fused_kernel(
    nt, nm, nz, g_hbm, gam_hbm, shift_hbm, off_hbm, coup_hbm, nbr_hbm, out_ref,
    g_ref, gam_ref, shift_ref, off_ref, coup_ref, nbr_ref, left, stage, held, fin, parts, tab,
    load_sem, a_send, a_recv, z_send, z_recv, near_send, near_recv, far_send, far_recv, own_sem,
):
    t, m, z = lax.axis_index("tile"), lax.axis_index("mom"), lax.axis_index("ewin")
    orb, width = g_hbm.shape
    tall = orb // nt
    qr = tall // nm // 2
    hq = qr // 2
    has_up, has_down = z < nz - 1, z > 0

    def dev(tt, mm, zz):
        return {"tile": tt, "mom": mm, "ewin": zz}

    def order(q):
        return q + (q // 2) * (5 - 2 * q)

    ring = order(t)

    def tile_at(i):
        return order(lax.rem(ring + i, nt))

    def tile_rows(tile):
        return pl.ds(pl.multiple_of(tile * tall, tall), tall)

    def load(i):
        rows = tile_rows(tile_at(i))
        return pltpu.make_async_copy(g_hbm.at[rows], g_ref.at[rows], load_sem.at[i])

    def mom_at(j):
        return lax.rem(m + j, nm)

    def share(mm):
        return lax.rem(mm + z, nm)

    mine = share(m)
    up_mom, down_mom = mom_at(nm - 1), mom_at(1 % nm)
    pairs = [(i, j) for i in range(nt) for j in range(nm)]
    barrier = pltpu.get_barrier_semaphore()
    for i, j in sorted(pairs[1:], key=lambda pair: pair[0] != nt // 2):
        pl.semaphore_signal(barrier, inc=1, device_id=dev(tile_at(i), mom_at(j), z), device_id_type=MESH)

    @pl.when(has_up)
    def _():
        pl.semaphore_signal(barrier, inc=1, device_id=dev(t, up_mom, z + 1), device_id_type=MESH)

    @pl.when(has_down)
    def _():
        pl.semaphore_signal(barrier, inc=1, device_id=dev(t, down_mom, z - 1), device_id_type=MESH)

    loads = [pltpu.make_async_copy(gam_hbm, gam_ref, load_sem.at[nt])]
    loads += [load(i) for i in (0, 2, 1, 3)]
    small = ((shift_hbm, shift_ref), (off_hbm, off_ref), (coup_hbm, coup_ref), (nbr_hbm, nbr_ref))
    small = [pltpu.make_async_copy(src, dst, load_sem.at[nt + 1 + n]) for n, (src, dst) in enumerate(small)]
    for copy in loads + small:
        copy.start()

    def times(slot, right):
        both = lax.dot_general(
            left[slot], right, (((1,), (1,)), ((), ())), preferred_element_type=jnp.float32
        )
        return both[:tall], both[tall:]

    def scale_rows(i):
        rows = g_ref[tile_rows(tile_at(i)), :]
        re = rows[:, :orb].astype(jnp.float32) * gam_ref[...]
        im = rows[:, orb:].astype(jnp.float32) * gam_ref[...]
        left[i, :tall, :orb] = re.astype(jnp.bfloat16)
        left[i, :tall, orb:] = im.astype(jnp.bfloat16)
        left[i, tall:, :orb] = im.astype(jnp.bfloat16)
        left[i, tall:, orb:] = (-re).astype(jnp.bfloat16)

    def triangle():
        return (lax.broadcasted_iota(jnp.int32, (tall, tall), d) for d in (0, 1))

    def put_cross(a):
        first, second = lax.rem(a - ring + nt, nt), lax.rem(a + 2 - ring + nt, nt)
        re, im = times(first, g_ref[tile_rows(order(a + 2)), :])
        re = re.reshape(2, nm, qr, tall).astype(jnp.bfloat16)
        im = im.reshape(2, nm, qr, tall).astype(jnp.bfloat16)
        for h, i in enumerate((first, second)):
            stage[i, :, 0, :, :tall] = re[h]
            stage[i, :, 0, :, tall:] = im[h]

    def put_pair(i):
        here, there = g_ref[tile_rows(tile_at(i)), :], g_ref[tile_rows(tile_at(i + 1)), :]
        re, im = times(i, jnp.concatenate([here, there], axis=0))
        row, col = triangle()
        both = jnp.where(row > col, im[:, :tall], re[:, :tall]).reshape(nm, 2, qr, tall).astype(jnp.bfloat16)
        stage[i, :, 3, :, :tall] = both[:, 0]
        stage[i, :, 3, :, tall:] = both[:, 1]
        for cols, block in ((slice(0, tall), re[:, tall:]), (slice(tall, 2 * tall), im[:, tall:])):
            block = block.reshape(2, nm, 2, hq, tall).astype(jnp.bfloat16)
            for h in range(2):
                for b in range(2):
                    stage[(i + h) % nt, :, 1 + b, h * hq : (h + 1) * hq, cols] = block[h, :, b]

    groups = ((0, 1), (1, 1), (2, 1), (3, 1))
    slots = (0, 1, 3, 2)

    def slot_of(i, j):
        return slots[i] * nm + j

    def a_copy(g, i, j):
        v, n = groups[g]
        to = mom_at(j)
        return pltpu.make_async_remote_copy(
            src_ref=stage.at[i, share(to), pl.ds(v, n)],
            dst_ref=held.at[1, pl.ds(v, n), slot_of(i, j)],
            send_sem=a_send.at[g, i, j],
            recv_sem=a_recv.at[g, i, j],
            device_id=dev(tile_at(i), to, z),
            device_id_type=MESH,
        )

    def own_copy():
        return pltpu.make_async_copy(stage.at[0, mine], held.at[1, pl.ds(0, 4), 0], own_sem)

    def send(g, i):
        for j in range(nm):
            if (i, j) != (0, 0):
                a_copy(g, i, j).start()

    def arrived(g, i):
        for j in range(nm):
            if (i, j) != (0, 0):
                a_copy(g, i, j).wait_recv()

    chunks = (
        (0, 1, 0, 1), (1, 3, 0, 1), (0, 4, 1, nm - 1),
        (0, 1, nm, 2 * nm), (0, 1, 3 * nm, nm),
        (1, 1, nm, 3 * nm), (2, 1, nm, 3 * nm), (3, 1, nm, 3 * nm),
    )
    needs = ((0, 2, 3, 4), (1, 5), (6,), (7,))

    def z_copy(k, up):
        v, n, s, w = chunks[k]
        side = 0 if up else 1
        if s == 0:
            src, dst = stage.at[0, mine, pl.ds(v, n)], held.at[2 * side, pl.ds(v, n), 0]
        else:
            src, dst = held.at[1, pl.ds(v, n), pl.ds(s, w)], held.at[2 * side, pl.ds(v, n), pl.ds(s, w)]
        return pltpu.make_async_remote_copy(
            src_ref=src,
            dst_ref=dst,
            send_sem=z_send.at[side, k],
            recv_sem=z_recv.at[side, k],
            device_id=dev(t, up_mom if up else down_mom, z + 1 if up else z - 1),
            device_id_type=MESH,
        )

    def pass_on(k):
        @pl.when(has_up)
        def _():
            z_copy(k, True).start()

        @pl.when(has_down)
        def _():
            z_copy(k, False).start()

    base = lax.rem(ring, 2)
    near, far = lax.rem(base - ring + nt, nt), lax.rem(1 - base - ring + nt, nt)
    for copy in loads[:3]:
        copy.wait()
    scale_rows(near)
    put_cross(base)
    for copy in loads[3:]:
        copy.wait()
    scale_rows(far)
    put_cross(1 - base)
    pl.semaphore_wait(barrier, nt * nm - 1 + has_up.astype(jnp.int32) + has_down.astype(jnp.int32))
    send(0, 2)
    send(0, 0)
    pass_on(0)
    send(0, 1)
    send(0, 3)
    scale_rows(lax.rem(near + 2, nt))
    scale_rows(lax.rem(far + 2, nt))
    put_pair(0)
    put_pair(3)
    for g in (1, 2, 3):
        send(g, 0)
    pass_on(1)
    own_copy().start()
    put_pair(1)
    send(1, 1)
    put_pair(2)
    for g, i in ((1, 2), (1, 3), (2, 2), (2, 1), (2, 3), (3, 2), (3, 1), (3, 3)):
        send(g, i)
    for g in range(4):
        arrived(g, 0)
    pass_on(2)
    for i in (1, 3):
        arrived(0, i)
    pass_on(3)
    arrived(0, 2)
    pass_on(4)

    @pl.when(jnp.logical_not(has_down))
    def _():
        held[0] = jnp.zeros(held.shape[1:], held.dtype)

    @pl.when(jnp.logical_not(has_up))
    def _():
        held[2] = jnp.zeros(held.shape[1:], held.dtype)

    for copy in small:
        copy.wait()
    shifts = [lax.rem(lax.rem(shift_ref[s], nm) + nm, nm) for s in range(shift_ref.shape[0])]
    table = []
    for diff in range(nm):
        per_off = []
        for o in range(NW):
            acc = jnp.float32(0.0)
            for s in range(len(shifts)):
                acc = acc + jnp.where(shifts[s] == diff, coup_ref[s, o], 0.0)
            per_off.append(acc)
        row = []
        for d in range(2 * HW + 1):
            acc = jnp.float32(0.0)
            for o in range(NW):
                acc = acc + jnp.where(off_ref[o] + HW == d, per_off[o], 0.0)
            row.append(acc)
        table.append(row)
    for d in range(2 * HW + 1):
        tab[0, d] = 0.5 * (table[0][d] + table[1][d])
        tab[1, d] = 0.5 * (table[0][d] - table[1][d])

    for i in (1, 3, 2):
        arrived(1, i)
    pass_on(5)
    own_copy().wait()

    bases = []
    for p in range(nt):
        i = lax.rem(ring - order(p) + nt, nt)
        bases.append((i + (i // 2) * (5 - 2 * i)) * nm)

    def block_lo(block, who):
        return pl.multiple_of((block * nm + share(who)) * qr, qr)

    def pieces(v, who, here):
        if v == 0:
            block = ring // 2 if here else 1 - ring // 2
            return [(0, qr, 2, block_lo(block, who), 2, 2)]
        if v == 3:
            return [(3 * qr, qr, 3, block_lo(0, who), None, None)]
        off = (v - 1) * hq
        return [
            (v * qr + h * hq, hq, h, pl.multiple_of(block_lo(h, who) + off, hq), 1 - h, 1 if h == 0 else nt - 1)
            for h in range(2)
        ]

    def near_copy(v, h, kk, who):
        lo, n, slot, row, _, _ = pieces(v, who, True)[h]
        return pltpu.make_async_remote_copy(
            src_ref=fin.at[kk, :, pl.ds(lo, n)],
            dst_ref=parts.at[slot, :, pl.ds(row, n)],
            send_sem=near_send.at[v, h, kk],
            recv_sem=near_recv.at[v, h, kk],
            device_id=dev(t, mom_at(kk), z),
            device_id_type=MESH,
        )

    def far_copy(v, h, kk, who, here):
        lo, n, _, row, slot, step = pieces(v, who, here)[h]
        return pltpu.make_async_remote_copy(
            src_ref=fin.at[kk, :, pl.ds(lo, n)],
            dst_ref=parts.at[slot, :, pl.ds(row, n)],
            send_sem=far_send.at[v, h, kk],
            recv_sem=far_recv.at[v, h, kk],
            device_id=dev(tile_at(step), mom_at(kk), z),
            device_id_type=MESH,
        )

    def halves(v):
        return range(2 if v in (1, 2) else 1)

    def mix(v):
        for k in needs[v]:
            @pl.when(has_down)
            def _():
                z_copy(k, True).wait_recv()

            @pl.when(has_up)
            def _():
                z_copy(k, False).wait_recv()

        own = pieces(v, m, True)
        weight = [[tab[part, d] for d in range(2 * HW + 1)] for part in range(2)]
        wide = 2 * tall // LANES
        for lo, n, slot, row, _, _ in own:
            for step in range(n // PACK * wide):
                r = step // wide * PACK
                inner = pl.ds(lo - v * qr + r, PACK)
                rows = pl.ds(lo + r, PACK)
                cols = pl.ds(step % wide * LANES, LANES)
                acc = [[None] * nt for _ in range(2)]
                for zs in range(3):
                    for p in range(nt):
                        src = zs * nt + p
                        x = [held[zs, v, bases[p] + (j + zs + 1) % 2, inner, cols].astype(jnp.float32) for j in range(2)]
                        for part, y in enumerate((x[0] + x[1], x[0] - x[1])):
                            for e in range(nt):
                                if 0 <= src - e <= 2 * HW:
                                    term = weight[part][src - e] * y
                                    acc[part][e] = term if acc[part][e] is None else acc[part][e] + term
                for e in range(nt):
                    for kk, value in enumerate((acc[0][e] + acc[1][e], acc[0][e] - acc[1][e])):
                        value = value.astype(jnp.bfloat16)
                        if kk == 0:
                            parts[slot, e, pl.ds(pl.multiple_of(row + r, PACK), PACK), cols] = value
                        if kk > 0 or v < 3:
                            fin[kk, e, rows, cols] = value

        for h in halves(v):
            for kk in range(nm):
                if v < 3:
                    far_copy(v, h, kk, m, True).start()
                if kk > 0:
                    near_copy(v, h, kk, m).start()

    def landed(v):
        for h in halves(v):
            for kk in range(nm):
                who = mom_at(nm - kk)
                if v < 3:
                    far_copy(v, h, kk, who, False).wait_recv()
                if kk > 0:
                    near_copy(v, h, kk, who).wait_recv()

    def kept(tile):
        found = jnp.float32(0.0)
        for b in range(nbr_ref.shape[1]):
            found = jnp.where(nbr_ref[t, b] == tile, 1.0, found)
        return found

    def store(part, tile, flip):
        keep = kept(tile)

        for e in range(nt):
            re, im = parts[part, e, :, :tall].astype(jnp.float32), parts[part, e, :, tall:].astype(jnp.float32)
            if flip:
                re, im = re.T, -im.T
            re, im = (re * keep).astype(jnp.bfloat16), (im * keep).astype(jnp.bfloat16)
            out_ref[e, :, pl.ds(pl.multiple_of(tile * tall, tall), tall)] = re
            out_ref[e, :, pl.ds(pl.multiple_of(orb + tile * tall, tall), tall)] = im

    def store_diagonal():
        row, col = triangle()
        keep = kept(t)

        for e in range(nt):
            packed = [
                parts[3, e, c * qr : (c + 1) * qr, h * tall : (h + 1) * tall] for c in range(nm) for h in range(2)
            ]
            both = jnp.concatenate(packed, axis=0).astype(jnp.float32)
            turned = both.T
            re = jnp.where(row > col, turned, both)
            im = jnp.where(row > col, both, jnp.where(row < col, -turned, 0.0))
            out_ref[e, :, pl.ds(pl.multiple_of(t * tall, tall), tall)] = (re * keep).astype(jnp.bfloat16)
            out_ref[e, :, pl.ds(pl.multiple_of(orb + t * tall, tall), tall)] = (im * keep).astype(jnp.bfloat16)

    for i in (1, 3, 2):
        arrived(2, i)
    pass_on(6)
    mix(0)
    for i in (1, 3, 2):
        arrived(3, i)
    pass_on(7)
    mix(1)
    mix(2)
    mix(3)
    landed(0)

    @pl.when(ring < 2)
    def _():
        store(2, tile_at(2), False)

    @pl.when(ring >= 2)
    def _():
        store(2, tile_at(2), True)

    landed(1)
    landed(2)
    store(0, tile_at(1), False)
    store(1, tile_at(nt - 1), True)
    landed(3)
    store_diagonal()

    for v in range(4):
        for h in halves(v):
            for kk in range(nm):
                if v < 3:
                    far_copy(v, h, kk, m, True).wait_send()
                if kk > 0:
                    near_copy(v, h, kk, m).wait_send()
    for i, j in pairs[1:]:
        for g in range(4):
            a_copy(g, i, j).wait_send()
    for k in range(len(chunks)):
        @pl.when(has_up)
        def _():
            z_copy(k, True).wait_send()

        @pl.when(has_down)
        def _():
            z_copy(k, False).wait_send()


def fused(green_ret, injection, mom_shift, phon_off, coupling, tile_nbr):
    nt, nm, nz = lax.axis_size("tile"), lax.axis_size("mom"), lax.axis_size("ewin")
    orbitals, width = green_ret.shape[3:]
    tall = orbitals // nt
    qr = tall // nm // 2
    green = green_ret.reshape(orbitals, width)
    gamma = injection.reshape(1, orbitals)
    vmem, anywhere = pl.BlockSpec(memory_space=pltpu.VMEM), pl.BlockSpec(memory_space=pl.ANY)
    args = (green, gamma, mom_shift, phon_off, coupling, tile_nbr)
    dma = pltpu.SemaphoreType.DMA
    total = pl.pallas_call(
        lambda *refs: fused_kernel(nt, nm, nz, *refs),
        out_shape=pltpu.VMEM((nt, tall, width), jnp.bfloat16),
        in_specs=[anywhere] * len(args),
        out_specs=vmem,
        scratch_shapes=[
            pltpu.VMEM(green.shape, green.dtype),
            pltpu.VMEM(gamma.shape, gamma.dtype),
            *[pltpu.SMEM(a.shape, a.dtype) for a in args[2:]],
            pltpu.VMEM((nt, 2 * tall, width), jnp.bfloat16),
            pltpu.VMEM((nt, nm, 4, qr, 2 * tall), jnp.bfloat16),
            pltpu.VMEM((3, 4, nt * nm, qr, 2 * tall), jnp.bfloat16),
            pltpu.VMEM((nm, nt, 4 * qr, 2 * tall), jnp.bfloat16),
            pltpu.VMEM((4, nt, tall, 2 * tall), jnp.bfloat16),
            pltpu.SMEM((nm, 2 * HW + 1), jnp.float32),
            dma((nt + 5,)),
            dma((4, nt, nm)),
            dma((4, nt, nm)),
            dma((2, 8)),
            dma((2, 8)),
            dma((4, 2, nm)),
            dma((4, 2, nm)),
            dma((4, 2, nm)),
            dma((4, 2, nm)),
            dma,
        ],
        compiler_params=pltpu.CompilerParams(collective_id=0, has_side_effects=True),
    )(*args)
    return total[None, None]


def with_halo(shard, sides, width):
    for axis, dim in sides:
        peers, length = (lax.axis_size(axis), shard.shape[dim])
        up = [(i, (i + 1) % peers) for i in range(peers - 1)]
        down = [(j, i) for i, j in up]
        last = lax.slice_in_dim(shard, length - width, length, axis=dim)
        initial = lax.slice_in_dim(shard, 0, width, axis=dim)
        before = lax.ppermute(last, axis, up)
        after = lax.ppermute(initial, axis, down)
        shard = jnp.concatenate([before, shard, after], axis=dim)
    return shard


def on_device(green_ret, injection, mom_shift, phon_off, coupling, tile_nbr):
    blocks = green_ret[0, 0]
    gamma = injection[0, 0]
    orbitals = blocks.shape[1]
    ntiles = lax.axis_size("tile")
    per_tile = orbitals // ntiles
    real_part = blocks[:, :, :orbitals].astype(jnp.float32)
    imag_part = blocks[:, :, orbitals:].astype(jnp.float32)
    scale = gamma[:, None, :]
    left_re = jnp.concatenate([real_part * scale, imag_part * scale], axis=2).astype(jnp.bfloat16)
    left_im = jnp.concatenate([imag_part * scale, -real_part * scale], axis=2).astype(jnp.bfloat16)
    real_out = jnp.einsum("prk,pck->prc", left_re, blocks, preferred_element_type=jnp.float32)
    imag_out = jnp.einsum("prk,pck->prc", left_im, blocks, preferred_element_type=jnp.float32)
    payload = jnp.concatenate([real_out, imag_out], axis=2).astype(jnp.bfloat16)
    exchanged = lax.all_to_all(payload, "tile", split_axis=1, concat_axis=0, tiled=True)
    energies = exchanged.shape[0]
    rimmed = with_halo(exchanged, (("ewin", 0),), HW)
    extended = lax.all_gather(rimmed[None], "mom", axis=0, tiled=True)
    nmom = lax.axis_size("mom")
    here = lax.axis_index("mom")
    source = jnp.mod(here - mom_shift, nmom)
    onehot = (source[:, None] == jnp.arange(nmom, dtype=jnp.int32)[None, :]).astype(jnp.float32)
    weights = jnp.dot(onehot.T, coupling, precision=lax.Precision.HIGHEST)
    total = jnp.zeros(exchanged.shape, jnp.float32)
    for offset in range(NW):
        start = HW + phon_off[offset]
        piece = lax.dynamic_slice_in_dim(extended, start, energies, 1)
        for moment in range(nmom):
            total = total + weights[moment, offset] * piece[moment].astype(jnp.float32)
    tile_here = lax.axis_index("tile")
    neighbours = lax.dynamic_index_in_dim(tile_nbr, tile_here, 0, keepdims=False)
    coltile = jnp.arange(orbitals, dtype=jnp.int32) // per_tile
    colmask = jnp.any(coltile[:, None] == neighbours[None, :], axis=1).astype(jnp.float32)
    colmask = jnp.concatenate([colmask, colmask])
    result = (total * colmask[None, None, :]).astype(jnp.bfloat16)
    return result[None, None]


def body_for(mesh):
    nt, nm = mesh.shape["tile"], mesh.shape["mom"]

    def body(green_ret, *rest):
        points, orbitals = green_ret.shape[2:4]
        aligned = orbitals % (nt * LANES) == 0 and orbitals % (nt * nm * 4 * PACK) == 0
        if aligned and points == 1 and nt == HW and nm == 2:
            return fused(green_ret, *rest)
        return on_device(green_ret, *rest)

    return body


def solution(mesh):
    placed = (
        P("mom", "ewin", "tile", None, None),
        P("mom", "ewin", "tile", None),
        P(),
        P(),
        P(),
        P(),
    )
    return jax.shard_map(
        body_for(mesh),
        mesh=mesh,
        in_specs=placed,
        out_specs=P("mom", "ewin", None, "tile", None),
        check_vma=False,
    )
```

```python
import jax
import jax.numpy as jnp
from jax import lax
from jax.experimental import pallas as pl
from jax.experimental.pallas import tpu as pltpu
from jax.sharding import PartitionSpec as P

HW = 4
NW = 8
LANES = 128
PACK = 16
MESH = pl.DeviceIdType.MESH


def fused_kernel(
    nt, nm, nz, g_hbm, gam_hbm, shift_hbm, off_hbm, coup_hbm, nbr_hbm, out_ref,
    g_ref, gam_ref, shift_ref, off_ref, coup_ref, nbr_ref, left, stage, held, fin, parts, tab,
    load_sem, a_send, a_recv, z_send, z_recv, near_send, far_send, mixed_recv, own_sem,
):
    t, m, z = lax.axis_index("tile"), lax.axis_index("mom"), lax.axis_index("ewin")
    orb, width = g_hbm.shape
    tall = orb // nt
    qr = tall // nm // 2
    hq = qr // 2
    has_up, has_down = z < nz - 1, z > 0

    def dev(tt, mm, zz):
        return {"tile": tt, "mom": mm, "ewin": zz}

    def order(q):
        return q + (q // 2) * (5 - 2 * q)

    ring = order(t)

    def tile_at(i):
        return order(lax.rem(ring + i, nt))

    def tile_rows(tile):
        return pl.ds(pl.multiple_of(tile * tall, tall), tall)

    def load(i):
        rows = tile_rows(tile_at(i))
        return pltpu.make_async_copy(g_hbm.at[rows], g_ref.at[rows], load_sem.at[i % 2])

    def mom_at(j):
        return lax.rem(m + j, nm)

    def share(mm):
        return lax.rem(mm + z, nm)

    mine = share(m)
    up_mom, down_mom = mom_at(nm - 1), mom_at(1 % nm)
    pairs = [(i, j) for i in range(nt) for j in range(nm)]
    barrier = pltpu.get_barrier_semaphore()
    for i, j in sorted(pairs[1:], key=lambda pair: pair[0] != nt // 2):
        pl.semaphore_signal(barrier, inc=1, device_id=dev(tile_at(i), mom_at(j), z), device_id_type=MESH)

    @pl.when(has_up)
    def _():
        pl.semaphore_signal(barrier, inc=1, device_id=dev(t, up_mom, z + 1), device_id_type=MESH)

    @pl.when(has_down)
    def _():
        pl.semaphore_signal(barrier, inc=1, device_id=dev(t, down_mom, z - 1), device_id_type=MESH)

    loads = [pltpu.make_async_copy(gam_hbm, gam_ref, load_sem.at[2])]
    loads += [load(i) for i in (0, 2, 1, 3)]
    small = ((shift_hbm, shift_ref), (off_hbm, off_ref), (coup_hbm, coup_ref), (nbr_hbm, nbr_ref))
    small = [pltpu.make_async_copy(src, dst, load_sem.at[3 + n]) for n, (src, dst) in enumerate(small)]
    for copy in loads + small:
        copy.start()

    def drained(ref, sem):
        pltpu.make_async_copy(ref, ref, sem).wait()

    def times(slot, right):
        both = lax.dot_general(
            left[slot], right, (((1,), (1,)), ((), ())), preferred_element_type=jnp.float32
        )
        return both[:tall], both[tall:]

    def scale_rows(i):
        rows = g_ref[tile_rows(tile_at(i)), :]
        re = rows[:, :orb].astype(jnp.float32) * gam_ref[...]
        im = rows[:, orb:].astype(jnp.float32) * gam_ref[...]
        left[i, :tall, :orb] = re.astype(jnp.bfloat16)
        left[i, :tall, orb:] = im.astype(jnp.bfloat16)
        left[i, tall:, :orb] = im.astype(jnp.bfloat16)
        left[i, tall:, orb:] = (-re).astype(jnp.bfloat16)

    def triangle():
        return (lax.broadcasted_iota(jnp.int32, (tall, tall), d) for d in (0, 1))

    def put_cross(a):
        first, second = lax.rem(a - ring + nt, nt), lax.rem(a + 2 - ring + nt, nt)
        re, im = times(first, g_ref[tile_rows(order(a + 2)), :])
        re = re.reshape(2, nm, qr, tall).astype(jnp.bfloat16)
        im = im.reshape(2, nm, qr, tall).astype(jnp.bfloat16)
        for h, i in enumerate((first, second)):
            stage[i, :, 0, :, :tall] = re[h]
            stage[i, :, 0, :, tall:] = im[h]

    def put_pair(i):
        here, there = g_ref[tile_rows(tile_at(i)), :], g_ref[tile_rows(tile_at(i + 1)), :]
        re, im = times(i, jnp.concatenate([here, there], axis=0))
        row, col = triangle()
        both = jnp.where(row > col, im[:, :tall], re[:, :tall]).reshape(nm, 2, qr, tall).astype(jnp.bfloat16)
        stage[i, :, 3, :, :tall] = both[:, 0]
        stage[i, :, 3, :, tall:] = both[:, 1]
        for cols, block in ((slice(0, tall), re[:, tall:]), (slice(tall, 2 * tall), im[:, tall:])):
            block = block.reshape(2, nm, 2, hq, tall).astype(jnp.bfloat16)
            for h in range(2):
                for b in range(2):
                    stage[(i + h) % nt, :, 1 + b, h * hq : (h + 1) * hq, cols] = block[h, :, b]

    groups = ((0, 1), (1, 1), (2, 1), (3, 1))
    slots = (0, 1, 3, 2)

    def slot_of(i, j):
        return slots[i] * nm + j

    arrivals = (
        (0, 4, 1, nm - 1), (0, 1, nm, 2 * nm), (0, 1, 3 * nm, nm),
        (1, 1, nm, 2 * nm), (1, 1, 3 * nm, nm), (2, 1, nm, 3 * nm), (3, 1, nm, 3 * nm),
    )

    def awaited(g, i):
        return 0 if i == 0 else (1, 3, 5, 6)[g] + (1 if i == 2 and g < 2 else 0)

    def a_copy(g, i, j):
        v, n = groups[g]
        to = mom_at(j)
        return pltpu.make_async_remote_copy(
            src_ref=stage.at[i, share(to), pl.ds(v, n)],
            dst_ref=held.at[1, pl.ds(v, n), slot_of(i, j)],
            send_sem=a_send.at[min(i, 1)],
            recv_sem=a_recv.at[awaited(g, i)],
            device_id=dev(tile_at(i), to, z),
            device_id_type=MESH,
        )

    def own_copy():
        return pltpu.make_async_copy(stage.at[0, mine], held.at[1, pl.ds(0, 4), 0], own_sem)

    def send(g, i):
        for j in range(nm):
            if (i, j) != (0, 0):
                a_copy(g, i, j).start()

    def arrived(n):
        v, units, slot, many = arrivals[n]
        drained(held.at[1, pl.ds(v, units), pl.ds(slot, many)], a_recv.at[n])

    chunks = (
        (0, 1, 0, 1), (1, 3, 0, 1), (0, 4, 1, nm - 1),
        (0, 1, nm, 2 * nm), (0, 1, 3 * nm, nm),
        (1, 1, nm, 2 * nm), (1, 1, 3 * nm, nm), (2, 1, nm, 3 * nm), (3, 1, nm, 3 * nm),
    )
    unit_of = (0, 0, 0, 0, 0, 1, 1, 2, 3)

    def z_copy(k, up):
        v, n, s, w = chunks[k]
        side = 0 if up else 1
        if s == 0:
            src, dst = stage.at[0, mine, pl.ds(v, n)], held.at[2 * side, pl.ds(v, n), 0]
        else:
            src, dst = held.at[1, pl.ds(v, n), pl.ds(s, w)], held.at[2 * side, pl.ds(v, n), pl.ds(s, w)]
        return pltpu.make_async_remote_copy(
            src_ref=src,
            dst_ref=dst,
            send_sem=z_send.at[side],
            recv_sem=z_recv.at[side, unit_of[k]],
            device_id=dev(t, up_mom if up else down_mom, z + 1 if up else z - 1),
            device_id_type=MESH,
        )

    def pass_on(k):
        @pl.when(has_up)
        def _():
            z_copy(k, True).start()

        @pl.when(has_down)
        def _():
            z_copy(k, False).start()

    base = lax.rem(ring, 2)
    near, far = lax.rem(base - ring + nt, nt), lax.rem(1 - base - ring + nt, nt)
    loads[0].wait()
    drained(g_ref.at[pl.ds(0, 2 * tall)], load_sem.at[0])
    scale_rows(near)
    put_cross(base)
    drained(g_ref.at[pl.ds(0, 2 * tall)], load_sem.at[1])
    scale_rows(far)
    put_cross(1 - base)
    pl.semaphore_wait(barrier, nt * nm - 1 + has_up.astype(jnp.int32) + has_down.astype(jnp.int32))
    pass_on(0)
    send(0, 1)
    send(0, 3)
    send(0, 0)
    send(0, 2)
    scale_rows(lax.rem(near + 2, nt))
    scale_rows(lax.rem(far + 2, nt))
    put_pair(0)
    put_pair(3)
    for g in (1, 2, 3):
        send(g, 0)
    pass_on(1)
    own_copy().start()
    put_pair(1)
    send(1, 1)
    put_pair(2)
    for g, i in ((1, 3), (1, 2), (2, 2), (2, 1), (2, 3), (3, 2), (3, 1), (3, 3)):
        send(g, i)
    for n in range(3):
        arrived(n)
        pass_on(2 + n)

    @pl.when(jnp.logical_not(has_down))
    def _():
        held[0] = jnp.zeros(held.shape[1:], held.dtype)

    @pl.when(jnp.logical_not(has_up))
    def _():
        held[2] = jnp.zeros(held.shape[1:], held.dtype)

    for copy in small:
        copy.wait()
    shifts = [lax.rem(lax.rem(shift_ref[s], nm) + nm, nm) for s in range(shift_ref.shape[0])]
    table = []
    for diff in range(nm):
        per_off = []
        for o in range(NW):
            acc = jnp.float32(0.0)
            for s in range(len(shifts)):
                acc = acc + jnp.where(shifts[s] == diff, coup_ref[s, o], 0.0)
            per_off.append(acc)
        row = []
        for d in range(2 * HW + 1):
            acc = jnp.float32(0.0)
            for o in range(NW):
                acc = acc + jnp.where(off_ref[o] + HW == d, per_off[o], 0.0)
            row.append(acc)
        table.append(row)
    for d in range(2 * HW + 1):
        tab[0, d] = 0.5 * (table[0][d] + table[1][d])
        tab[1, d] = 0.5 * (table[0][d] - table[1][d])

    for n in (3, 4):
        arrived(n)
        pass_on(2 + n)
    own_copy().wait()

    bases = []
    for p in range(nt):
        i = lax.rem(ring - order(p) + nt, nt)
        bases.append((i + (i // 2) * (5 - 2 * i)) * nm)

    def block_lo(block, who):
        return pl.multiple_of((block * nm + share(who)) * qr, qr)

    def pieces(v, who, here):
        if v == 0:
            block = ring // 2 if here else 1 - ring // 2
            return [(0, qr, 2, block_lo(block, who), 2, 2)]
        if v == 3:
            return [(3 * qr, qr, 3, block_lo(0, who), None, None)]
        off = (v - 1) * hq
        return [
            (v * qr + h * hq, hq, h, pl.multiple_of(block_lo(h, who) + off, hq), 1 - h, 1 if h == 0 else nt - 1)
            for h in range(2)
        ]

    def near_copy(v, h, kk, who):
        lo, n, slot, row, _, _ = pieces(v, who, True)[h]
        return pltpu.make_async_remote_copy(
            src_ref=fin.at[kk, :, pl.ds(lo, n)],
            dst_ref=parts.at[slot, :, pl.ds(row, n)],
            send_sem=near_send,
            recv_sem=mixed_recv.at[(v + 1) // 2],
            device_id=dev(t, mom_at(kk), z),
            device_id_type=MESH,
        )

    def far_copy(v, h, kk, who, here):
        lo, n, _, row, slot, step = pieces(v, who, here)[h]
        return pltpu.make_async_remote_copy(
            src_ref=fin.at[kk, :, pl.ds(lo, n)],
            dst_ref=parts.at[slot, :, pl.ds(row, n)],
            send_sem=far_send,
            recv_sem=mixed_recv.at[(v + 1) // 2],
            device_id=dev(tile_at(step), mom_at(kk), z),
            device_id_type=MESH,
        )

    def halves(v):
        return range(2 if v in (1, 2) else 1)

    def mix(v):
        for side, there in enumerate((has_down, has_up)):
            @pl.when(there)
            def _():
                got = held.at[2 * side]
                got = got.at[pl.ds(0, nm), pl.ds(0, 7)] if v == 0 else got.at[v, pl.ds(nm, 3 * nm)]
                drained(got, z_recv.at[side, v])

        own = pieces(v, m, True)
        weight = [[tab[part, d] for d in range(2 * HW + 1)] for part in range(2)]
        wide = 2 * tall // LANES
        for lo, n, slot, row, _, _ in own:
            for step in range(n // PACK * wide):
                r = step // wide * PACK
                inner = pl.ds(lo - v * qr + r, PACK)
                rows = pl.ds(lo + r, PACK)
                cols = pl.ds(step % wide * LANES, LANES)
                acc = [[None] * nt for _ in range(2)]
                for zs in range(3):
                    for p in range(nt):
                        src = zs * nt + p
                        x = [held[zs, v, bases[p] + (j + zs + 1) % 2, inner, cols].astype(jnp.float32) for j in range(2)]
                        for part, y in enumerate((x[0] + x[1], x[0] - x[1])):
                            for e in range(nt):
                                if 0 <= src - e <= 2 * HW:
                                    term = weight[part][src - e] * y
                                    acc[part][e] = term if acc[part][e] is None else acc[part][e] + term
                for e in range(nt):
                    for kk, value in enumerate((acc[0][e] + acc[1][e], acc[0][e] - acc[1][e])):
                        value = value.astype(jnp.bfloat16)
                        if kk == 0:
                            parts[slot, e, pl.ds(pl.multiple_of(row + r, PACK), PACK), cols] = value
                        if kk > 0 or v < 3:
                            fin[kk, e, rows, cols] = value

        for h in halves(v):
            for kk in range(nm):
                if v < 3:
                    far_copy(v, h, kk, m, True).start()
                if kk > 0:
                    near_copy(v, h, kk, m).start()

    def landed(n):
        copies, rows = ((2 * nm - 1, qr), (2 * nm - 1, 2 * qr), (nm - 1, qr))[n]
        drained(parts.at[pl.ds(0, copies), :, pl.ds(0, rows)], mixed_recv.at[n])

    def kept(tile):
        found = jnp.float32(0.0)
        for b in range(nbr_ref.shape[1]):
            found = jnp.where(nbr_ref[t, b] == tile, 1.0, found)
        return found

    def store(part, tile, flip):
        keep = kept(tile)

        for e in range(nt):
            re, im = parts[part, e, :, :tall].astype(jnp.float32), parts[part, e, :, tall:].astype(jnp.float32)
            if flip:
                re, im = re.T, -im.T
            re, im = (re * keep).astype(jnp.bfloat16), (im * keep).astype(jnp.bfloat16)
            out_ref[e, :, pl.ds(pl.multiple_of(tile * tall, tall), tall)] = re
            out_ref[e, :, pl.ds(pl.multiple_of(orb + tile * tall, tall), tall)] = im

    def store_diagonal():
        row, col = triangle()
        keep = kept(t)

        for e in range(nt):
            packed = [
                parts[3, e, c * qr : (c + 1) * qr, h * tall : (h + 1) * tall] for c in range(nm) for h in range(2)
            ]
            both = jnp.concatenate(packed, axis=0).astype(jnp.float32)
            turned = both.T
            re = jnp.where(row > col, turned, both)
            im = jnp.where(row > col, both, jnp.where(row < col, -turned, 0.0))
            out_ref[e, :, pl.ds(pl.multiple_of(t * tall, tall), tall)] = (re * keep).astype(jnp.bfloat16)
            out_ref[e, :, pl.ds(pl.multiple_of(orb + t * tall, tall), tall)] = (im * keep).astype(jnp.bfloat16)

    arrived(5)
    pass_on(7)
    mix(0)
    arrived(6)
    pass_on(8)
    drained(stage.at[0, pl.ds(0, nm - 1)], a_send.at[0])
    drained(stage.at[pl.ds(1, nt - 1)], a_send.at[1])
    for v in range(1, 4):
        mix(v)
    landed(0)

    @pl.when(ring < 2)
    def _():
        store(2, tile_at(2), False)

    @pl.when(ring >= 2)
    def _():
        store(2, tile_at(2), True)

    for side, there in enumerate((has_up, has_down)):
        @pl.when(there)
        def _():
            drained(held.at[1], z_send.at[side])

    drained(fin.at[:, :, pl.ds(0, 3 * qr)], far_send)
    landed(1)
    store(0, tile_at(1), False)
    store(1, tile_at(nt - 1), True)
    drained(fin.at[pl.ds(1, nm - 1)], near_send)
    landed(2)
    store_diagonal()


def fused(green_ret, injection, mom_shift, phon_off, coupling, tile_nbr):
    nt, nm, nz = lax.axis_size("tile"), lax.axis_size("mom"), lax.axis_size("ewin")
    orbitals, width = green_ret.shape[3:]
    tall = orbitals // nt
    qr = tall // nm // 2
    green = green_ret.reshape(orbitals, width)
    gamma = injection.reshape(1, orbitals)
    vmem, anywhere = pl.BlockSpec(memory_space=pltpu.VMEM), pl.BlockSpec(memory_space=pl.ANY)
    args = (green, gamma, mom_shift, phon_off, coupling, tile_nbr)
    dma = pltpu.SemaphoreType.DMA
    total = pl.pallas_call(
        lambda *refs: fused_kernel(nt, nm, nz, *refs),
        out_shape=pltpu.VMEM((nt, tall, width), jnp.bfloat16),
        in_specs=[anywhere] * len(args),
        out_specs=vmem,
        scratch_shapes=[
            pltpu.VMEM(green.shape, green.dtype),
            pltpu.VMEM(gamma.shape, gamma.dtype),
            *[pltpu.SMEM(a.shape, a.dtype) for a in args[2:]],
            pltpu.VMEM((nt, 2 * tall, width), jnp.bfloat16),
            pltpu.VMEM((nt, nm, 4, qr, 2 * tall), jnp.bfloat16),
            pltpu.VMEM((3, 4, nt * nm, qr, 2 * tall), jnp.bfloat16),
            pltpu.VMEM((nm, nt, 4 * qr, 2 * tall), jnp.bfloat16),
            pltpu.VMEM((4, nt, tall, 2 * tall), jnp.bfloat16),
            pltpu.SMEM((nm, 2 * HW + 1), jnp.float32),
            dma((7,)),
            dma((2,)),
            dma((7,)),
            dma((2,)),
            dma((2, 4)),
            dma,
            dma,
            dma((3,)),
            dma,
        ],
        compiler_params=pltpu.CompilerParams(collective_id=0, has_side_effects=True),
    )(*args)
    return total[None, None]


def with_halo(shard, sides, width):
    for axis, dim in sides:
        peers, length = (lax.axis_size(axis), shard.shape[dim])
        up = [(i, (i + 1) % peers) for i in range(peers - 1)]
        down = [(j, i) for i, j in up]
        last = lax.slice_in_dim(shard, length - width, length, axis=dim)
        initial = lax.slice_in_dim(shard, 0, width, axis=dim)
        before = lax.ppermute(last, axis, up)
        after = lax.ppermute(initial, axis, down)
        shard = jnp.concatenate([before, shard, after], axis=dim)
    return shard


def on_device(green_ret, injection, mom_shift, phon_off, coupling, tile_nbr):
    blocks = green_ret[0, 0]
    gamma = injection[0, 0]
    orbitals = blocks.shape[1]
    ntiles = lax.axis_size("tile")
    per_tile = orbitals // ntiles
    real_part = blocks[:, :, :orbitals].astype(jnp.float32)
    imag_part = blocks[:, :, orbitals:].astype(jnp.float32)
    scale = gamma[:, None, :]
    left_re = jnp.concatenate([real_part * scale, imag_part * scale], axis=2).astype(jnp.bfloat16)
    left_im = jnp.concatenate([imag_part * scale, -real_part * scale], axis=2).astype(jnp.bfloat16)
    real_out = jnp.einsum("prk,pck->prc", left_re, blocks, preferred_element_type=jnp.float32)
    imag_out = jnp.einsum("prk,pck->prc", left_im, blocks, preferred_element_type=jnp.float32)
    payload = jnp.concatenate([real_out, imag_out], axis=2).astype(jnp.bfloat16)
    exchanged = lax.all_to_all(payload, "tile", split_axis=1, concat_axis=0, tiled=True)
    energies = exchanged.shape[0]
    rimmed = with_halo(exchanged, (("ewin", 0),), HW)
    extended = lax.all_gather(rimmed[None], "mom", axis=0, tiled=True)
    nmom = lax.axis_size("mom")
    here = lax.axis_index("mom")
    source = jnp.mod(here - mom_shift, nmom)
    onehot = (source[:, None] == jnp.arange(nmom, dtype=jnp.int32)[None, :]).astype(jnp.float32)
    weights = jnp.dot(onehot.T, coupling, precision=lax.Precision.HIGHEST)
    total = jnp.zeros(exchanged.shape, jnp.float32)
    for offset in range(NW):
        start = HW + phon_off[offset]
        piece = lax.dynamic_slice_in_dim(extended, start, energies, 1)
        for moment in range(nmom):
            total = total + weights[moment, offset] * piece[moment].astype(jnp.float32)
    tile_here = lax.axis_index("tile")
    neighbours = lax.dynamic_index_in_dim(tile_nbr, tile_here, 0, keepdims=False)
    coltile = jnp.arange(orbitals, dtype=jnp.int32) // per_tile
    colmask = jnp.any(coltile[:, None] == neighbours[None, :], axis=1).astype(jnp.float32)
    colmask = jnp.concatenate([colmask, colmask])
    result = (total * colmask[None, None, :]).astype(jnp.bfloat16)
    return result[None, None]


def body_for(mesh):
    nt, nm = mesh.shape["tile"], mesh.shape["mom"]

    def body(green_ret, *rest):
        points, orbitals = green_ret.shape[2:4]
        aligned = orbitals % (nt * LANES) == 0 and orbitals % (nt * nm * 4 * PACK) == 0
        if aligned and points == 1 and nt == HW and nm == 2:
            return fused(green_ret, *rest)
        return on_device(green_ret, *rest)

    return body


def solution(mesh):
    placed = (
        P("mom", "ewin", "tile", None, None),
        P("mom", "ewin", "tile", None),
        P(),
        P(),
        P(),
        P(),
    )
    return jax.shard_map(
        body_for(mesh),
        mesh=mesh,
        in_specs=placed,
        out_specs=P("mom", "ewin", None, "tile", None),
        check_vma=False,
    )
```

```python
import jax
import jax.numpy as jnp
from jax import lax
from jax.experimental import pallas as pl
from jax.experimental.pallas import tpu as pltpu
from jax.sharding import PartitionSpec as P

HW = 4
NW = 8
LANES = 128
PACK = 16
MESH = pl.DeviceIdType.MESH


def fused_kernel(
    nt, nm, nz, g_hbm, gam_hbm, shift_hbm, off_hbm, coup_hbm, nbr_hbm, out_ref,
    g_ref, gam_ref, shift_ref, off_ref, coup_ref, nbr_ref, left, stage, held, fin, parts, tab,
    load_sem, a_send, a_recv, z_send, z_recv, near_send, far_send, mixed_recv, own_sem,
):
    t, m, z = lax.axis_index("tile"), lax.axis_index("mom"), lax.axis_index("ewin")
    orb, width = g_hbm.shape
    tall = orb // nt
    qr = tall // nm // 2
    hq = qr // 2
    has_up, has_down = z < nz - 1, z > 0

    def dev(tt, mm, zz):
        return {"tile": tt, "mom": mm, "ewin": zz}

    def order(q):
        return q + (q // 2) * (5 - 2 * q)

    ring = order(t)

    def tile_at(i):
        return order(lax.rem(ring + i, nt))

    def tile_rows(tile):
        return pl.ds(pl.multiple_of(tile * tall, tall), tall)

    def load(i):
        rows = tile_rows(tile_at(i))
        return pltpu.make_async_copy(g_hbm.at[rows], g_ref.at[rows], load_sem.at[i % 2])

    def mom_at(j):
        return lax.rem(m + j, nm)

    def share(mm):
        return lax.rem(mm + z, nm)

    mine = share(m)
    up_mom, down_mom = mom_at(nm - 1), mom_at(1 % nm)
    pairs = [(i, j) for i in range(nt) for j in range(nm)]
    barrier = pltpu.get_barrier_semaphore()
    for i, j in sorted(pairs[1:], key=lambda pair: pair[0] != nt // 2):
        pl.semaphore_signal(barrier, inc=1, device_id=dev(tile_at(i), mom_at(j), z), device_id_type=MESH)

    @pl.when(has_up)
    def _():
        pl.semaphore_signal(barrier, inc=1, device_id=dev(t, up_mom, z + 1), device_id_type=MESH)

    @pl.when(has_down)
    def _():
        pl.semaphore_signal(barrier, inc=1, device_id=dev(t, down_mom, z - 1), device_id_type=MESH)

    loads = [pltpu.make_async_copy(gam_hbm, gam_ref, load_sem.at[2])]
    loads += [load(i) for i in (0, 2, 1, 3)]
    small = ((shift_hbm, shift_ref), (off_hbm, off_ref), (coup_hbm, coup_ref), (nbr_hbm, nbr_ref))
    small = [pltpu.make_async_copy(src, dst, load_sem.at[3 + n]) for n, (src, dst) in enumerate(small)]
    for copy in loads + small:
        copy.start()

    def drained(ref, sem):
        pltpu.make_async_copy(ref, ref, sem).wait()

    def times(slot, right):
        both = lax.dot_general(
            left[slot], right, (((1,), (1,)), ((), ())), preferred_element_type=jnp.float32
        )
        return both[:tall], both[tall:]

    def scale_rows(i):
        rows = g_ref[tile_rows(tile_at(i)), :]
        re = rows[:, :orb].astype(jnp.float32) * gam_ref[...]
        im = rows[:, orb:].astype(jnp.float32) * gam_ref[...]
        left[i, :tall, :orb] = re.astype(jnp.bfloat16)
        left[i, :tall, orb:] = im.astype(jnp.bfloat16)
        left[i, tall:, :orb] = im.astype(jnp.bfloat16)
        left[i, tall:, orb:] = (-re).astype(jnp.bfloat16)

    def triangle():
        return (lax.broadcasted_iota(jnp.int32, (tall, tall), d) for d in (0, 1))

    def put_cross(a):
        first, second = lax.rem(a - ring + nt, nt), lax.rem(a + 2 - ring + nt, nt)
        re, im = times(first, g_ref[tile_rows(order(a + 2)), :])
        re = re.reshape(2, nm, qr, tall).astype(jnp.bfloat16)
        im = im.reshape(2, nm, qr, tall).astype(jnp.bfloat16)
        for h, i in enumerate((first, second)):
            stage[i, :, 0, :, :tall] = re[h]
            stage[i, :, 0, :, tall:] = im[h]

    def put_pair(i):
        here, there = g_ref[tile_rows(tile_at(i)), :], g_ref[tile_rows(tile_at(i + 1)), :]
        re, im = times(i, jnp.concatenate([here, there], axis=0))
        row, col = triangle()
        both = jnp.where(row > col, im[:, :tall], re[:, :tall]).reshape(nm, 2, qr, tall).astype(jnp.bfloat16)
        stage[i, :, 3, :, :tall] = both[:, 0]
        stage[i, :, 3, :, tall:] = both[:, 1]
        for cols, block in ((slice(0, tall), re[:, tall:]), (slice(tall, 2 * tall), im[:, tall:])):
            block = block.reshape(2, nm, 2, hq, tall).astype(jnp.bfloat16)
            for h in range(2):
                for b in range(2):
                    stage[(i + h) % nt, :, 1 + b, h * hq : (h + 1) * hq, cols] = block[h, :, b]

    groups = ((0, 1), (1, 1), (2, 1), (3, 1))
    slots = (0, 1, 3, 2)

    def slot_of(i, j):
        return slots[i] * nm + j

    arrivals = (
        (0, 4, 1, nm - 1), (0, 1, nm, 2 * nm), (0, 1, 3 * nm, nm),
        (1, 1, nm, 2 * nm), (1, 1, 3 * nm, nm), (2, 1, nm, 3 * nm), (3, 1, nm, 3 * nm),
    )

    def awaited(g, i):
        return 0 if i == 0 else (1, 3, 5, 6)[g] + (1 if i == 2 and g < 2 else 0)

    def a_copy(g, i, j):
        v, n = groups[g]
        to = mom_at(j)
        return pltpu.make_async_remote_copy(
            src_ref=stage.at[i, share(to), pl.ds(v, n)],
            dst_ref=held.at[1, pl.ds(v, n), slot_of(i, j)],
            send_sem=a_send.at[min(i, 1)],
            recv_sem=a_recv.at[awaited(g, i)],
            device_id=dev(tile_at(i), to, z),
            device_id_type=MESH,
        )

    def own_copy():
        return pltpu.make_async_copy(stage.at[0, mine], held.at[1, pl.ds(0, 4), 0], own_sem)

    def send(g, i):
        for j in range(nm):
            if (i, j) != (0, 0):
                a_copy(g, i, j).start()

    def arrived(n):
        v, units, slot, many = arrivals[n]
        drained(held.at[1, pl.ds(v, units), pl.ds(slot, many)], a_recv.at[n])

    chunks = (
        (0, 1, 0, 1), (1, 3, 0, 1), (0, 4, 1, nm - 1),
        (0, 1, nm, 2 * nm), (0, 1, 3 * nm, nm),
        (1, 1, nm, 2 * nm), (1, 1, 3 * nm, nm), (2, 1, nm, 3 * nm), (3, 1, nm, 3 * nm),
    )
    unit_of = (0, 0, 0, 0, 0, 1, 1, 2, 3)

    def z_copy(k, up):
        v, n, s, w = chunks[k]
        side = 0 if up else 1
        if s == 0:
            src, dst = stage.at[0, mine, pl.ds(v, n)], held.at[2 * side, pl.ds(v, n), 0]
        else:
            src, dst = held.at[1, pl.ds(v, n), pl.ds(s, w)], held.at[2 * side, pl.ds(v, n), pl.ds(s, w)]
        return pltpu.make_async_remote_copy(
            src_ref=src,
            dst_ref=dst,
            send_sem=z_send.at[side],
            recv_sem=z_recv.at[side, unit_of[k]],
            device_id=dev(t, up_mom if up else down_mom, z + 1 if up else z - 1),
            device_id_type=MESH,
        )

    def pass_on(k):
        @pl.when(has_up)
        def _():
            z_copy(k, True).start()

        @pl.when(has_down)
        def _():
            z_copy(k, False).start()

    base = lax.rem(ring, 2)
    near, far = lax.rem(base - ring + nt, nt), lax.rem(1 - base - ring + nt, nt)
    loads[0].wait()
    drained(g_ref.at[pl.ds(0, 2 * tall)], load_sem.at[0])
    scale_rows(near)
    put_cross(base)
    drained(g_ref.at[pl.ds(0, 2 * tall)], load_sem.at[1])
    scale_rows(far)
    put_cross(1 - base)
    pl.semaphore_wait(barrier, nt * nm - 1 + has_up.astype(jnp.int32) + has_down.astype(jnp.int32))
    pass_on(0)
    send(0, 0)
    send(0, 1)
    send(0, 3)
    send(0, 2)
    scale_rows(lax.rem(near + 2, nt))
    scale_rows(lax.rem(far + 2, nt))
    put_pair(0)
    put_pair(3)
    for g in (1, 2, 3):
        send(g, 0)
    pass_on(1)
    own_copy().start()
    put_pair(1)
    send(1, 1)
    put_pair(2)
    for g, i in ((1, 3), (1, 2), (2, 2), (2, 1), (2, 3), (3, 2), (3, 1), (3, 3)):
        send(g, i)
    for n in range(3):
        arrived(n)
        pass_on(2 + n)

    @pl.when(jnp.logical_not(has_down))
    def _():
        held[0] = jnp.zeros(held.shape[1:], held.dtype)

    @pl.when(jnp.logical_not(has_up))
    def _():
        held[2] = jnp.zeros(held.shape[1:], held.dtype)

    for copy in small:
        copy.wait()
    shifts = [lax.rem(lax.rem(shift_ref[s], nm) + nm, nm) for s in range(shift_ref.shape[0])]
    table = []
    for diff in range(nm):
        per_off = []
        for o in range(NW):
            acc = jnp.float32(0.0)
            for s in range(len(shifts)):
                acc = acc + jnp.where(shifts[s] == diff, coup_ref[s, o], 0.0)
            per_off.append(acc)
        row = []
        for d in range(2 * HW + 1):
            acc = jnp.float32(0.0)
            for o in range(NW):
                acc = acc + jnp.where(off_ref[o] + HW == d, per_off[o], 0.0)
            row.append(acc)
        table.append(row)
    for d in range(2 * HW + 1):
        tab[0, d] = 0.5 * (table[0][d] + table[1][d])
        tab[1, d] = 0.5 * (table[0][d] - table[1][d])

    for n in (3, 4):
        arrived(n)
        pass_on(2 + n)
    own_copy().wait()

    bases = []
    for p in range(nt):
        i = lax.rem(ring - order(p) + nt, nt)
        bases.append((i + (i // 2) * (5 - 2 * i)) * nm)

    def block_lo(block, who):
        return pl.multiple_of((block * nm + share(who)) * qr, qr)

    def pieces(v, who, here):
        if v == 0:
            block = ring // 2 if here else 1 - ring // 2
            return [(0, qr, 2, block_lo(block, who), 2, 2)]
        if v == 3:
            return [(3 * qr, qr, 3, block_lo(0, who), None, None)]
        off = (v - 1) * hq
        return [
            (v * qr + h * hq, hq, h, pl.multiple_of(block_lo(h, who) + off, hq), 1 - h, 1 if h == 0 else nt - 1)
            for h in range(2)
        ]

    def near_copy(v, h, kk, who):
        lo, n, slot, row, _, _ = pieces(v, who, True)[h]
        return pltpu.make_async_remote_copy(
            src_ref=fin.at[kk, :, pl.ds(lo, n)],
            dst_ref=parts.at[slot, :, pl.ds(row, n)],
            send_sem=near_send,
            recv_sem=mixed_recv.at[(v + 1) // 2],
            device_id=dev(t, mom_at(kk), z),
            device_id_type=MESH,
        )

    def far_copy(v, h, kk, who, here):
        lo, n, _, row, slot, step = pieces(v, who, here)[h]
        return pltpu.make_async_remote_copy(
            src_ref=fin.at[kk, :, pl.ds(lo, n)],
            dst_ref=parts.at[slot, :, pl.ds(row, n)],
            send_sem=far_send,
            recv_sem=mixed_recv.at[(v + 1) // 2],
            device_id=dev(tile_at(step), mom_at(kk), z),
            device_id_type=MESH,
        )

    def halves(v):
        return range(2 if v in (1, 2) else 1)

    def mix(v):
        for side, there in enumerate((has_down, has_up)):
            @pl.when(there)
            def _():
                got = held.at[2 * side]
                got = got.at[pl.ds(0, nm), pl.ds(0, 7)] if v == 0 else got.at[v, pl.ds(nm, 3 * nm)]
                drained(got, z_recv.at[side, v])

        own = pieces(v, m, True)
        weight = [[tab[part, d] for d in range(2 * HW + 1)] for part in range(2)]
        wide = 2 * tall // LANES
        for lo, n, slot, row, _, _ in own:
            for step in range(n // PACK * wide):
                r = step // wide * PACK
                inner = pl.ds(lo - v * qr + r, PACK)
                rows = pl.ds(lo + r, PACK)
                cols = pl.ds(step % wide * LANES, LANES)
                acc = [[None] * nt for _ in range(2)]
                for zs in range(3):
                    for p in range(nt):
                        src = zs * nt + p
                        x = [held[zs, v, bases[p] + (j + zs + 1) % 2, inner, cols].astype(jnp.float32) for j in range(2)]
                        for part, y in enumerate((x[0] + x[1], x[0] - x[1])):
                            for e in range(nt):
                                if 0 <= src - e <= 2 * HW:
                                    term = weight[part][src - e] * y
                                    acc[part][e] = term if acc[part][e] is None else acc[part][e] + term
                for e in range(nt):
                    for kk, value in enumerate((acc[0][e] + acc[1][e], acc[0][e] - acc[1][e])):
                        value = value.astype(jnp.bfloat16)
                        if kk == 0:
                            parts[slot, e, pl.ds(pl.multiple_of(row + r, PACK), PACK), cols] = value
                        if kk > 0 or v < 3:
                            fin[kk, e, rows, cols] = value

        for h in halves(v):
            for kk in range(nm):
                if v < 3:
                    far_copy(v, h, kk, m, True).start()
                if kk > 0:
                    near_copy(v, h, kk, m).start()

    def landed(n):
        copies, rows = ((2 * nm - 1, qr), (2 * nm - 1, 2 * qr), (nm - 1, qr))[n]
        drained(parts.at[pl.ds(0, copies), :, pl.ds(0, rows)], mixed_recv.at[n])

    def kept(tile):
        found = jnp.float32(0.0)
        for b in range(nbr_ref.shape[1]):
            found = jnp.where(nbr_ref[t, b] == tile, 1.0, found)
        return found

    def store(part, tile, flip):
        keep = kept(tile)

        for e in range(nt):
            re, im = parts[part, e, :, :tall].astype(jnp.float32), parts[part, e, :, tall:].astype(jnp.float32)
            if flip:
                re, im = re.T, -im.T
            re, im = (re * keep).astype(jnp.bfloat16), (im * keep).astype(jnp.bfloat16)
            out_ref[e, :, pl.ds(pl.multiple_of(tile * tall, tall), tall)] = re
            out_ref[e, :, pl.ds(pl.multiple_of(orb + tile * tall, tall), tall)] = im

    def store_diagonal():
        row, col = triangle()
        keep = kept(t)

        for e in range(nt):
            packed = [
                parts[3, e, c * qr : (c + 1) * qr, h * tall : (h + 1) * tall] for c in range(nm) for h in range(2)
            ]
            both = jnp.concatenate(packed, axis=0).astype(jnp.float32)
            turned = both.T
            re = jnp.where(row > col, turned, both)
            im = jnp.where(row > col, both, jnp.where(row < col, -turned, 0.0))
            out_ref[e, :, pl.ds(pl.multiple_of(t * tall, tall), tall)] = (re * keep).astype(jnp.bfloat16)
            out_ref[e, :, pl.ds(pl.multiple_of(orb + t * tall, tall), tall)] = (im * keep).astype(jnp.bfloat16)

    arrived(5)
    pass_on(7)
    arrived(6)
    pass_on(8)
    mix(0)
    drained(stage.at[0, pl.ds(0, nm - 1)], a_send.at[0])
    drained(stage.at[pl.ds(1, nt - 1)], a_send.at[1])
    for v in range(1, 4):
        mix(v)
    landed(0)

    @pl.when(ring < 2)
    def _():
        store(2, tile_at(2), False)

    @pl.when(ring >= 2)
    def _():
        store(2, tile_at(2), True)

    for side, there in enumerate((has_up, has_down)):
        @pl.when(there)
        def _():
            drained(held.at[1], z_send.at[side])

    drained(fin.at[:, :, pl.ds(0, 3 * qr)], far_send)
    landed(2)
    store_diagonal()
    drained(fin.at[pl.ds(1, nm - 1)], near_send)
    landed(1)
    store(0, tile_at(1), False)
    store(1, tile_at(nt - 1), True)


def fused(green_ret, injection, mom_shift, phon_off, coupling, tile_nbr):
    nt, nm, nz = lax.axis_size("tile"), lax.axis_size("mom"), lax.axis_size("ewin")
    orbitals, width = green_ret.shape[3:]
    tall = orbitals // nt
    qr = tall // nm // 2
    green = green_ret.reshape(orbitals, width)
    gamma = injection.reshape(1, orbitals)
    vmem, anywhere = pl.BlockSpec(memory_space=pltpu.VMEM), pl.BlockSpec(memory_space=pl.ANY)
    args = (green, gamma, mom_shift, phon_off, coupling, tile_nbr)
    dma = pltpu.SemaphoreType.DMA
    total = pl.pallas_call(
        lambda *refs: fused_kernel(nt, nm, nz, *refs),
        out_shape=pltpu.VMEM((nt, tall, width), jnp.bfloat16),
        in_specs=[anywhere] * len(args),
        out_specs=vmem,
        scratch_shapes=[
            pltpu.VMEM(green.shape, green.dtype),
            pltpu.VMEM(gamma.shape, gamma.dtype),
            *[pltpu.SMEM(a.shape, a.dtype) for a in args[2:]],
            pltpu.VMEM((nt, 2 * tall, width), jnp.bfloat16),
            pltpu.VMEM((nt, nm, 4, qr, 2 * tall), jnp.bfloat16),
            pltpu.VMEM((3, 4, nt * nm, qr, 2 * tall), jnp.bfloat16),
            pltpu.VMEM((nm, nt, 4 * qr, 2 * tall), jnp.bfloat16),
            pltpu.VMEM((4, nt, tall, 2 * tall), jnp.bfloat16),
            pltpu.SMEM((nm, 2 * HW + 1), jnp.float32),
            dma((7,)),
            dma((2,)),
            dma((7,)),
            dma((2,)),
            dma((2, 4)),
            dma,
            dma,
            dma((3,)),
            dma,
        ],
        compiler_params=pltpu.CompilerParams(collective_id=0, has_side_effects=True),
    )(*args)
    return total[None, None]


def with_halo(shard, sides, width):
    for axis, dim in sides:
        peers, length = (lax.axis_size(axis), shard.shape[dim])
        up = [(i, (i + 1) % peers) for i in range(peers - 1)]
        down = [(j, i) for i, j in up]
        last = lax.slice_in_dim(shard, length - width, length, axis=dim)
        initial = lax.slice_in_dim(shard, 0, width, axis=dim)
        before = lax.ppermute(last, axis, up)
        after = lax.ppermute(initial, axis, down)
        shard = jnp.concatenate([before, shard, after], axis=dim)
    return shard


def on_device(green_ret, injection, mom_shift, phon_off, coupling, tile_nbr):
    blocks = green_ret[0, 0]
    gamma = injection[0, 0]
    orbitals = blocks.shape[1]
    ntiles = lax.axis_size("tile")
    per_tile = orbitals // ntiles
    real_part = blocks[:, :, :orbitals].astype(jnp.float32)
    imag_part = blocks[:, :, orbitals:].astype(jnp.float32)
    scale = gamma[:, None, :]
    left_re = jnp.concatenate([real_part * scale, imag_part * scale], axis=2).astype(jnp.bfloat16)
    left_im = jnp.concatenate([imag_part * scale, -real_part * scale], axis=2).astype(jnp.bfloat16)
    real_out = jnp.einsum("prk,pck->prc", left_re, blocks, preferred_element_type=jnp.float32)
    imag_out = jnp.einsum("prk,pck->prc", left_im, blocks, preferred_element_type=jnp.float32)
    payload = jnp.concatenate([real_out, imag_out], axis=2).astype(jnp.bfloat16)
    exchanged = lax.all_to_all(payload, "tile", split_axis=1, concat_axis=0, tiled=True)
    energies = exchanged.shape[0]
    rimmed = with_halo(exchanged, (("ewin", 0),), HW)
    extended = lax.all_gather(rimmed[None], "mom", axis=0, tiled=True)
    nmom = lax.axis_size("mom")
    here = lax.axis_index("mom")
    source = jnp.mod(here - mom_shift, nmom)
    onehot = (source[:, None] == jnp.arange(nmom, dtype=jnp.int32)[None, :]).astype(jnp.float32)
    weights = jnp.dot(onehot.T, coupling, precision=lax.Precision.HIGHEST)
    total = jnp.zeros(exchanged.shape, jnp.float32)
    for offset in range(NW):
        start = HW + phon_off[offset]
        piece = lax.dynamic_slice_in_dim(extended, start, energies, 1)
        for moment in range(nmom):
            total = total + weights[moment, offset] * piece[moment].astype(jnp.float32)
    tile_here = lax.axis_index("tile")
    neighbours = lax.dynamic_index_in_dim(tile_nbr, tile_here, 0, keepdims=False)
    coltile = jnp.arange(orbitals, dtype=jnp.int32) // per_tile
    colmask = jnp.any(coltile[:, None] == neighbours[None, :], axis=1).astype(jnp.float32)
    colmask = jnp.concatenate([colmask, colmask])
    result = (total * colmask[None, None, :]).astype(jnp.bfloat16)
    return result[None, None]


def body_for(mesh):
    nt, nm = mesh.shape["tile"], mesh.shape["mom"]

    def body(green_ret, *rest):
        points, orbitals = green_ret.shape[2:4]
        aligned = orbitals % (nt * LANES) == 0 and orbitals % (nt * nm * 4 * PACK) == 0
        if aligned and points == 1 and nt == HW and nm == 2:
            return fused(green_ret, *rest)
        return on_device(green_ret, *rest)

    return body


def solution(mesh):
    placed = (
        P("mom", "ewin", "tile", None, None),
        P("mom", "ewin", "tile", None),
        P(),
        P(),
        P(),
        P(),
    )
    return jax.shard_map(
        body_for(mesh),
        mesh=mesh,
        in_specs=placed,
        out_specs=P("mom", "ewin", None, "tile", None),
        check_vma=False,
    )
```

```python
import jax
import jax.numpy as jnp
from jax import lax
from jax.experimental import pallas as pl
from jax.experimental.pallas import tpu as pltpu
from jax.sharding import PartitionSpec as P

HW = 4
NW = 8
LANES = 128
PACK = 16
MESH = pl.DeviceIdType.MESH


def fused_kernel(
    nt, nm, nz, g_hbm, gam_hbm, shift_hbm, off_hbm, coup_hbm, nbr_hbm, out_ref,
    g_ref, gam_ref, shift_ref, off_ref, coup_ref, nbr_ref, left, stage, held, fin, parts, tab,
    load_sem, a_send, a_recv, z_send, z_recv, near_send, far_send, mixed_recv, own_sem,
):
    t, m, z = lax.axis_index("tile"), lax.axis_index("mom"), lax.axis_index("ewin")
    orb, width = g_hbm.shape
    tall = orb // nt
    qr = tall // nm // 2
    hq = qr // 2
    has_up, has_down = z < nz - 1, z > 0

    def dev(tt, mm, zz):
        return {"tile": tt, "mom": mm, "ewin": zz}

    def order(q):
        return q + (q // 2) * (5 - 2 * q)

    ring = order(t)

    def tile_at(i):
        return order(lax.rem(ring + i, nt))

    def tile_rows(tile):
        return pl.ds(pl.multiple_of(tile * tall, tall), tall)

    def load(i):
        rows = tile_rows(tile_at(i))
        return pltpu.make_async_copy(g_hbm.at[rows], g_ref.at[rows], load_sem.at[i % 2])

    def mom_at(j):
        return lax.rem(m + j, nm)

    def share(mm):
        return lax.rem(mm + z, nm)

    mine = share(m)
    up_mom, down_mom = mom_at(nm - 1), mom_at(1 % nm)
    pairs = [(i, j) for i in range(nt) for j in range(nm)]
    barrier = pltpu.get_barrier_semaphore()
    for i, j in sorted(pairs[1:], key=lambda pair: pair[0] != nt // 2):
        pl.semaphore_signal(barrier, inc=1, device_id=dev(tile_at(i), mom_at(j), z), device_id_type=MESH)

    @pl.when(has_up)
    def _():
        pl.semaphore_signal(barrier, inc=1, device_id=dev(t, up_mom, z + 1), device_id_type=MESH)

    @pl.when(has_down)
    def _():
        pl.semaphore_signal(barrier, inc=1, device_id=dev(t, down_mom, z - 1), device_id_type=MESH)

    loads = [pltpu.make_async_copy(gam_hbm, gam_ref, load_sem.at[2])]
    loads += [load(i) for i in (0, 2, 1, 3)]
    small = ((shift_hbm, shift_ref), (off_hbm, off_ref), (coup_hbm, coup_ref), (nbr_hbm, nbr_ref))
    small = [pltpu.make_async_copy(src, dst, load_sem.at[3 + n]) for n, (src, dst) in enumerate(small)]
    for copy in loads + small:
        copy.start()

    def drained(ref, sem):
        pltpu.make_async_copy(ref, ref, sem).wait()

    def times(slot, right):
        both = lax.dot_general(
            left[slot], right, (((1,), (1,)), ((), ())), preferred_element_type=jnp.float32
        )
        return both[:tall], both[tall:]

    def scale_rows(i):
        rows = g_ref[tile_rows(tile_at(i)), :]
        re = rows[:, :orb].astype(jnp.float32) * gam_ref[...]
        im = rows[:, orb:].astype(jnp.float32) * gam_ref[...]
        left[i, :tall, :orb] = re.astype(jnp.bfloat16)
        left[i, :tall, orb:] = im.astype(jnp.bfloat16)
        left[i, tall:, :orb] = im.astype(jnp.bfloat16)
        left[i, tall:, orb:] = (-re).astype(jnp.bfloat16)

    def triangle():
        return (lax.broadcasted_iota(jnp.int32, (tall, tall), d) for d in (0, 1))

    def put_cross(a):
        first, second = lax.rem(a - ring + nt, nt), lax.rem(a + 2 - ring + nt, nt)
        re, im = times(first, g_ref[tile_rows(order(a + 2)), :])
        re = re.reshape(2, nm, qr, tall).astype(jnp.bfloat16)
        im = im.reshape(2, nm, qr, tall).astype(jnp.bfloat16)
        for h, i in enumerate((first, second)):
            stage[i, :, 0, :, :tall] = re[h]
            stage[i, :, 0, :, tall:] = im[h]

    def put_pair(i):
        here, there = g_ref[tile_rows(tile_at(i)), :], g_ref[tile_rows(tile_at(i + 1)), :]
        re, im = times(i, jnp.concatenate([here, there], axis=0))
        row, col = triangle()
        both = jnp.where(row > col, im[:, :tall], re[:, :tall]).reshape(nm, 2, qr, tall).astype(jnp.bfloat16)
        stage[i, :, 3, :, :tall] = both[:, 0]
        stage[i, :, 3, :, tall:] = both[:, 1]
        for cols, block in ((slice(0, tall), re[:, tall:]), (slice(tall, 2 * tall), im[:, tall:])):
            block = block.reshape(2, nm, 2, hq, tall).astype(jnp.bfloat16)
            for h in range(2):
                for b in range(2):
                    stage[(i + h) % nt, :, 1 + b, h * hq : (h + 1) * hq, cols] = block[h, :, b]

    groups = ((0, 1), (1, 1), (2, 1), (3, 1), (1, 3))
    slots = (0, 1, 3, 2)

    def slot_of(i, j):
        return slots[i] * nm + j

    arrivals = (
        (0, 4, 1, nm - 1), (0, 1, nm, 2 * nm), (0, 1, 3 * nm, nm),
        (1, 1, nm, 2 * nm), (1, 1, 3 * nm, nm), (2, 1, nm, 3 * nm), (3, 1, nm, 3 * nm),
    )

    def awaited(g, i):
        return 0 if i == 0 else (1, 3, 5, 6)[g] + (1 if i == 2 and g < 2 else 0)

    def a_copy(g, i, j):
        v, n = groups[g]
        to = mom_at(j)
        return pltpu.make_async_remote_copy(
            src_ref=stage.at[i, share(to), pl.ds(v, n)],
            dst_ref=held.at[1, pl.ds(v, n), slot_of(i, j)],
            send_sem=a_send,
            recv_sem=a_recv.at[awaited(g, i)],
            device_id=dev(tile_at(i), to, z),
            device_id_type=MESH,
        )

    def own_copy():
        return pltpu.make_async_copy(stage.at[0, mine], held.at[1, pl.ds(0, 4), 0], own_sem)

    def send(g, i):
        for j in range(nm):
            if (i, j) != (0, 0):
                a_copy(g, i, j).start()

    def arrived(n):
        v, units, slot, many = arrivals[n]
        drained(held.at[1, pl.ds(v, units), pl.ds(slot, many)], a_recv.at[n])

    chunks = (
        (0, 1, 0, 1), (1, 3, 0, 1), (0, 4, 1, nm - 1),
        (0, 1, nm, 2 * nm), (0, 1, 3 * nm, nm),
        (1, 1, nm, 2 * nm), (1, 1, 3 * nm, nm), (2, 1, nm, 3 * nm), (3, 1, nm, 3 * nm),
    )
    unit_of = (0, 0, 0, 0, 0, 1, 1, 2, 3)

    def z_copy(k, up):
        v, n, s, w = chunks[k]
        side = 0 if up else 1
        if s == 0:
            src, dst = stage.at[0, mine, pl.ds(v, n)], held.at[2 * side, pl.ds(v, n), 0]
        else:
            src, dst = held.at[1, pl.ds(v, n), pl.ds(s, w)], held.at[2 * side, pl.ds(v, n), pl.ds(s, w)]
        return pltpu.make_async_remote_copy(
            src_ref=src,
            dst_ref=dst,
            send_sem=z_send.at[side],
            recv_sem=z_recv.at[side, unit_of[k]],
            device_id=dev(t, up_mom if up else down_mom, z + 1 if up else z - 1),
            device_id_type=MESH,
        )

    def pass_on(k):
        @pl.when(has_up)
        def _():
            z_copy(k, True).start()

        @pl.when(has_down)
        def _():
            z_copy(k, False).start()

    base = lax.rem(ring, 2)
    near, far = lax.rem(base - ring + nt, nt), lax.rem(1 - base - ring + nt, nt)
    loads[0].wait()
    drained(g_ref.at[pl.ds(0, 2 * tall)], load_sem.at[0])
    scale_rows(near)
    put_cross(base)
    drained(g_ref.at[pl.ds(0, 2 * tall)], load_sem.at[1])
    scale_rows(far)
    put_cross(1 - base)
    pl.semaphore_wait(barrier, nt * nm - 1 + has_up.astype(jnp.int32) + has_down.astype(jnp.int32))
    pass_on(0)
    send(0, 0)
    send(0, 1)
    send(0, 3)
    send(0, 2)
    scale_rows(lax.rem(near + 2, nt))
    scale_rows(lax.rem(far + 2, nt))
    put_pair(0)
    put_pair(3)
    send(4, 0)
    pass_on(1)
    own_copy().start()
    put_pair(1)
    send(1, 1)
    put_pair(2)
    for g, i in ((1, 3), (1, 2), (2, 2), (2, 1), (2, 3), (3, 2), (3, 1), (3, 3)):
        send(g, i)
    for n in range(3):
        arrived(n)
        pass_on(2 + n)

    @pl.when(jnp.logical_not(has_down))
    def _():
        held[0] = jnp.zeros(held.shape[1:], held.dtype)

    @pl.when(jnp.logical_not(has_up))
    def _():
        held[2] = jnp.zeros(held.shape[1:], held.dtype)

    for copy in small:
        copy.wait()
    shifts = [lax.rem(lax.rem(shift_ref[s], nm) + nm, nm) for s in range(shift_ref.shape[0])]
    table = []
    for diff in range(nm):
        per_off = []
        for o in range(NW):
            acc = jnp.float32(0.0)
            for s in range(len(shifts)):
                acc = acc + jnp.where(shifts[s] == diff, coup_ref[s, o], 0.0)
            per_off.append(acc)
        row = []
        for d in range(2 * HW + 1):
            acc = jnp.float32(0.0)
            for o in range(NW):
                acc = acc + jnp.where(off_ref[o] + HW == d, per_off[o], 0.0)
            row.append(acc)
        table.append(row)
    for d in range(2 * HW + 1):
        tab[0, d] = 0.5 * (table[0][d] + table[1][d])
        tab[1, d] = 0.5 * (table[0][d] - table[1][d])

    for n in (3, 4):
        arrived(n)
        pass_on(2 + n)
    own_copy().wait()

    bases = []
    for p in range(nt):
        i = lax.rem(ring - order(p) + nt, nt)
        bases.append((i + (i // 2) * (5 - 2 * i)) * nm)

    def block_lo(block, who):
        return pl.multiple_of((block * nm + share(who)) * qr, qr)

    def pieces(v, who, here):
        if v == 0:
            block = ring // 2 if here else 1 - ring // 2
            return [(0, qr, 2, block_lo(block, who), 2, 2)]
        if v == 3:
            return [(3 * qr, qr, 3, block_lo(0, who), None, None)]
        off = (v - 1) * hq
        return [
            (v * qr + h * hq, hq, h, pl.multiple_of(block_lo(h, who) + off, hq), 1 - h, 1 if h == 0 else nt - 1)
            for h in range(2)
        ]

    def near_copy(v, h, kk, who):
        lo, n, slot, row, _, _ = pieces(v, who, True)[h]
        return pltpu.make_async_remote_copy(
            src_ref=fin.at[kk, :, pl.ds(lo, n)],
            dst_ref=parts.at[slot, :, pl.ds(row, n)],
            send_sem=near_send,
            recv_sem=mixed_recv.at[(v + 1) // 2],
            device_id=dev(t, mom_at(kk), z),
            device_id_type=MESH,
        )

    def far_copy(v, h, kk, who, here):
        lo, n, _, row, slot, step = pieces(v, who, here)[h]
        return pltpu.make_async_remote_copy(
            src_ref=fin.at[kk, :, pl.ds(lo, n)],
            dst_ref=parts.at[slot, :, pl.ds(row, n)],
            send_sem=far_send,
            recv_sem=mixed_recv.at[(v + 1) // 2],
            device_id=dev(tile_at(step), mom_at(kk), z),
            device_id_type=MESH,
        )

    def halves(v):
        return range(2 if v in (1, 2) else 1)

    def mix(v):
        for side, there in enumerate((has_down, has_up)):
            @pl.when(there)
            def _():
                got = held.at[2 * side]
                got = got.at[pl.ds(0, nm), pl.ds(0, 7)] if v == 0 else got.at[v, pl.ds(nm, 3 * nm)]
                drained(got, z_recv.at[side, v])

        own = pieces(v, m, True)
        weight = [[tab[part, d] for d in range(2 * HW + 1)] for part in range(2)]
        wide = 2 * tall // LANES
        for lo, n, slot, row, _, _ in own:
            for step in range(n // PACK * wide):
                r = step // wide * PACK
                inner = pl.ds(lo - v * qr + r, PACK)
                rows = pl.ds(lo + r, PACK)
                cols = pl.ds(step % wide * LANES, LANES)
                acc = [[None] * nt for _ in range(2)]
                for zs in range(3):
                    for p in range(nt):
                        src = zs * nt + p
                        x = [held[zs, v, bases[p] + (j + zs + 1) % 2, inner, cols].astype(jnp.float32) for j in range(2)]
                        for part, y in enumerate((x[0] + x[1], x[0] - x[1])):
                            for e in range(nt):
                                if 0 <= src - e <= 2 * HW:
                                    term = weight[part][src - e] * y
                                    acc[part][e] = term if acc[part][e] is None else acc[part][e] + term
                for e in range(nt):
                    for kk, value in enumerate((acc[0][e] + acc[1][e], acc[0][e] - acc[1][e])):
                        value = value.astype(jnp.bfloat16)
                        if kk == 0:
                            parts[slot, e, pl.ds(pl.multiple_of(row + r, PACK), PACK), cols] = value
                        if kk > 0 or v < 3:
                            fin[kk, e, rows, cols] = value

        if v < 3:
            for h in halves(v):
                for kk in range(nm):
                    far_copy(v, h, kk, m, True).start()
        for h in halves(v):
            for kk in range(1, nm):
                near_copy(v, h, kk, m).start()

    def landed(n):
        copies, rows = ((2 * nm - 1, qr), (2 * nm - 1, 2 * qr), (nm - 1, qr))[n]
        drained(parts.at[pl.ds(0, copies), :, pl.ds(0, rows)], mixed_recv.at[n])

    def kept(tile):
        found = jnp.float32(0.0)
        for b in range(nbr_ref.shape[1]):
            found = jnp.where(nbr_ref[t, b] == tile, 1.0, found)
        return found

    def store(part, tile, flip):
        keep = kept(tile)

        for e in range(nt):
            re, im = parts[part, e, :, :tall].astype(jnp.float32), parts[part, e, :, tall:].astype(jnp.float32)
            if flip:
                re, im = re.T, -im.T
            re, im = (re * keep).astype(jnp.bfloat16), (im * keep).astype(jnp.bfloat16)
            out_ref[e, :, pl.ds(pl.multiple_of(tile * tall, tall), tall)] = re
            out_ref[e, :, pl.ds(pl.multiple_of(orb + tile * tall, tall), tall)] = im

    def store_diagonal():
        row, col = triangle()
        keep = kept(t)

        for e in range(nt):
            packed = [
                parts[3, e, c * qr : (c + 1) * qr, h * tall : (h + 1) * tall] for c in range(nm) for h in range(2)
            ]
            both = jnp.concatenate(packed, axis=0).astype(jnp.float32)
            turned = both.T
            re = jnp.where(row > col, turned, both)
            im = jnp.where(row > col, both, jnp.where(row < col, -turned, 0.0))
            out_ref[e, :, pl.ds(pl.multiple_of(t * tall, tall), tall)] = (re * keep).astype(jnp.bfloat16)
            out_ref[e, :, pl.ds(pl.multiple_of(orb + t * tall, tall), tall)] = (im * keep).astype(jnp.bfloat16)

    arrived(5)
    pass_on(7)
    arrived(6)
    pass_on(8)
    mix(0)
    drained(held.at[1, pl.ds(0, 4), pl.ds(0, nt * nm - 1)], a_send)
    for v in range(1, 4):
        mix(v)
    landed(0)

    @pl.when(ring < 2)
    def _():
        store(2, tile_at(2), False)

    @pl.when(ring >= 2)
    def _():
        store(2, tile_at(2), True)

    for side, there in enumerate((has_up, has_down)):
        @pl.when(there)
        def _():
            drained(held.at[1], z_send.at[side])

    drained(fin.at[:, :, pl.ds(0, 3 * qr)], far_send)
    landed(2)
    store_diagonal()
    drained(fin.at[pl.ds(1, nm - 1)], near_send)
    landed(1)
    store(1, tile_at(nt - 1), True)
    store(0, tile_at(1), False)


def fused(green_ret, injection, mom_shift, phon_off, coupling, tile_nbr):
    nt, nm, nz = lax.axis_size("tile"), lax.axis_size("mom"), lax.axis_size("ewin")
    orbitals, width = green_ret.shape[3:]
    tall = orbitals // nt
    qr = tall // nm // 2
    green = green_ret.reshape(orbitals, width)
    gamma = injection.reshape(1, orbitals)
    vmem, anywhere = pl.BlockSpec(memory_space=pltpu.VMEM), pl.BlockSpec(memory_space=pl.ANY)
    args = (green, gamma, mom_shift, phon_off, coupling, tile_nbr)
    dma = pltpu.SemaphoreType.DMA
    total = pl.pallas_call(
        lambda *refs: fused_kernel(nt, nm, nz, *refs),
        out_shape=pltpu.VMEM((nt, tall, width), jnp.bfloat16),
        in_specs=[anywhere] * len(args),
        out_specs=vmem,
        scratch_shapes=[
            pltpu.VMEM(green.shape, green.dtype),
            pltpu.VMEM(gamma.shape, gamma.dtype),
            *[pltpu.SMEM(a.shape, a.dtype) for a in args[2:]],
            pltpu.VMEM((nt, 2 * tall, width), jnp.bfloat16),
            pltpu.VMEM((nt, nm, 4, qr, 2 * tall), jnp.bfloat16),
            pltpu.VMEM((3, 4, nt * nm, qr, 2 * tall), jnp.bfloat16),
            pltpu.VMEM((nm, nt, 4 * qr, 2 * tall), jnp.bfloat16),
            pltpu.VMEM((4, nt, tall, 2 * tall), jnp.bfloat16),
            pltpu.SMEM((nm, 2 * HW + 1), jnp.float32),
            dma((7,)),
            dma,
            dma((7,)),
            dma((2,)),
            dma((2, 4)),
            dma,
            dma,
            dma((3,)),
            dma,
        ],
        compiler_params=pltpu.CompilerParams(collective_id=0, has_side_effects=True),
    )(*args)
    return total[None, None]


def with_halo(shard, sides, width):
    for axis, dim in sides:
        peers, length = (lax.axis_size(axis), shard.shape[dim])
        up = [(i, (i + 1) % peers) for i in range(peers - 1)]
        down = [(j, i) for i, j in up]
        last = lax.slice_in_dim(shard, length - width, length, axis=dim)
        initial = lax.slice_in_dim(shard, 0, width, axis=dim)
        before = lax.ppermute(last, axis, up)
        after = lax.ppermute(initial, axis, down)
        shard = jnp.concatenate([before, shard, after], axis=dim)
    return shard


def on_device(green_ret, injection, mom_shift, phon_off, coupling, tile_nbr):
    blocks = green_ret[0, 0]
    gamma = injection[0, 0]
    orbitals = blocks.shape[1]
    ntiles = lax.axis_size("tile")
    per_tile = orbitals // ntiles
    real_part = blocks[:, :, :orbitals].astype(jnp.float32)
    imag_part = blocks[:, :, orbitals:].astype(jnp.float32)
    scale = gamma[:, None, :]
    left_re = jnp.concatenate([real_part * scale, imag_part * scale], axis=2).astype(jnp.bfloat16)
    left_im = jnp.concatenate([imag_part * scale, -real_part * scale], axis=2).astype(jnp.bfloat16)
    real_out = jnp.einsum("prk,pck->prc", left_re, blocks, preferred_element_type=jnp.float32)
    imag_out = jnp.einsum("prk,pck->prc", left_im, blocks, preferred_element_type=jnp.float32)
    payload = jnp.concatenate([real_out, imag_out], axis=2).astype(jnp.bfloat16)
    exchanged = lax.all_to_all(payload, "tile", split_axis=1, concat_axis=0, tiled=True)
    energies = exchanged.shape[0]
    rimmed = with_halo(exchanged, (("ewin", 0),), HW)
    extended = lax.all_gather(rimmed[None], "mom", axis=0, tiled=True)
    nmom = lax.axis_size("mom")
    here = lax.axis_index("mom")
    source = jnp.mod(here - mom_shift, nmom)
    onehot = (source[:, None] == jnp.arange(nmom, dtype=jnp.int32)[None, :]).astype(jnp.float32)
    weights = jnp.dot(onehot.T, coupling, precision=lax.Precision.HIGHEST)
    total = jnp.zeros(exchanged.shape, jnp.float32)
    for offset in range(NW):
        start = HW + phon_off[offset]
        piece = lax.dynamic_slice_in_dim(extended, start, energies, 1)
        for moment in range(nmom):
            total = total + weights[moment, offset] * piece[moment].astype(jnp.float32)
    tile_here = lax.axis_index("tile")
    neighbours = lax.dynamic_index_in_dim(tile_nbr, tile_here, 0, keepdims=False)
    coltile = jnp.arange(orbitals, dtype=jnp.int32) // per_tile
    colmask = jnp.any(coltile[:, None] == neighbours[None, :], axis=1).astype(jnp.float32)
    colmask = jnp.concatenate([colmask, colmask])
    result = (total * colmask[None, None, :]).astype(jnp.bfloat16)
    return result[None, None]


def body_for(mesh):
    nt, nm = mesh.shape["tile"], mesh.shape["mom"]

    def body(green_ret, *rest):
        points, orbitals = green_ret.shape[2:4]
        aligned = orbitals % (nt * LANES) == 0 and orbitals % (nt * nm * 4 * PACK) == 0
        if aligned and points == 1 and nt == HW and nm == 2:
            return fused(green_ret, *rest)
        return on_device(green_ret, *rest)

    return body


def solution(mesh):
    placed = (
        P("mom", "ewin", "tile", None, None),
        P("mom", "ewin", "tile", None),
        P(),
        P(),
        P(),
        P(),
    )
    return jax.shard_map(
        body_for(mesh),
        mesh=mesh,
        in_specs=placed,
        out_specs=P("mom", "ewin", None, "tile", None),
        check_vma=False,
    )
```

```python
import jax
import jax.numpy as jnp
from jax import lax
from jax.experimental import pallas as pl
from jax.experimental.pallas import tpu as pltpu
from jax.sharding import PartitionSpec as P

HW = 4
NW = 8
LANES = 128
PACK = 16
MESH = pl.DeviceIdType.MESH


def fused_kernel(
    nt, nm, nz, g_hbm, gam_hbm, shift_hbm, off_hbm, coup_hbm, nbr_hbm, out_ref,
    g_ref, gam_ref, shift_ref, off_ref, coup_ref, nbr_ref, left, stage, held, fin, parts, tab,
    load_sem, a_send, a_recv, z_send, z_recv, near_send, far_send, mixed_recv, own_sem,
):
    t, m, z = lax.axis_index("tile"), lax.axis_index("mom"), lax.axis_index("ewin")
    orb, width = g_hbm.shape
    tall = orb // nt
    qr = tall // nm // 2
    hq = qr // 2
    has_up, has_down = z < nz - 1, z > 0

    def dev(tt, mm, zz):
        return {"tile": tt, "mom": mm, "ewin": zz}

    def order(q):
        return q + (q // 2) * (5 - 2 * q)

    ring = order(t)

    def tile_at(i):
        return order(lax.rem(ring + i, nt))

    def tile_rows(tile):
        return pl.ds(pl.multiple_of(tile * tall, tall), tall)

    def load(i):
        rows = tile_rows(tile_at(i))
        return pltpu.make_async_copy(g_hbm.at[rows], g_ref.at[rows], load_sem.at[i % 2])

    def mom_at(j):
        return lax.rem(m + j, nm)

    def share(mm):
        return lax.rem(mm + z, nm)

    mine = share(m)
    up_mom, down_mom = mom_at(nm - 1), mom_at(1 % nm)
    pairs = [(i, j) for i in range(nt) for j in range(nm)]
    barrier = pltpu.get_barrier_semaphore()
    for i, j in sorted(pairs[1:], key=lambda pair: pair[0] != nt // 2):
        pl.semaphore_signal(barrier, inc=1, device_id=dev(tile_at(i), mom_at(j), z), device_id_type=MESH)

    @pl.when(has_up)
    def _():
        pl.semaphore_signal(barrier, inc=1, device_id=dev(t, up_mom, z + 1), device_id_type=MESH)

    @pl.when(has_down)
    def _():
        pl.semaphore_signal(barrier, inc=1, device_id=dev(t, down_mom, z - 1), device_id_type=MESH)

    loads = [pltpu.make_async_copy(gam_hbm, gam_ref, load_sem.at[2])]
    loads += [load(i) for i in (0, 2, 1, 3)]
    small = ((shift_hbm, shift_ref), (off_hbm, off_ref), (coup_hbm, coup_ref), (nbr_hbm, nbr_ref))
    small = [pltpu.make_async_copy(src, dst, load_sem.at[3 + n]) for n, (src, dst) in enumerate(small)]
    for copy in loads + small:
        copy.start()

    def drained(ref, sem):
        pltpu.make_async_copy(ref, ref, sem).wait()

    def times(slot, right):
        both = lax.dot_general(
            left[slot], right, (((1,), (1,)), ((), ())), preferred_element_type=jnp.float32
        )
        return both[:tall], both[tall:]

    def scale_rows(i):
        rows = g_ref[tile_rows(tile_at(i)), :]
        re = rows[:, :orb].astype(jnp.float32) * gam_ref[...]
        im = rows[:, orb:].astype(jnp.float32) * gam_ref[...]
        left[i, :tall, :orb] = re.astype(jnp.bfloat16)
        left[i, :tall, orb:] = im.astype(jnp.bfloat16)
        left[i, tall:, :orb] = im.astype(jnp.bfloat16)
        left[i, tall:, orb:] = (-re).astype(jnp.bfloat16)

    def triangle():
        return (lax.broadcasted_iota(jnp.int32, (tall, tall), d) for d in (0, 1))

    def put_cross(a):
        first, second = lax.rem(a - ring + nt, nt), lax.rem(a + 2 - ring + nt, nt)
        re, im = times(first, g_ref[tile_rows(order(a + 2)), :])
        re = re.reshape(2, nm, qr, tall).astype(jnp.bfloat16)
        im = im.reshape(2, nm, qr, tall).astype(jnp.bfloat16)
        for h, i in enumerate((first, second)):
            stage[i, :, 0, :, :tall] = re[h]
            stage[i, :, 0, :, tall:] = im[h]

    def put_pair(i):
        here, there = g_ref[tile_rows(tile_at(i)), :], g_ref[tile_rows(tile_at(i + 1)), :]
        re, im = times(i, jnp.concatenate([here, there], axis=0))
        row, col = triangle()
        both = jnp.where(row > col, im[:, :tall], re[:, :tall]).reshape(nm, 2, qr, tall).astype(jnp.bfloat16)
        stage[i, :, 3, :, :tall] = both[:, 0]
        stage[i, :, 3, :, tall:] = both[:, 1]
        for cols, block in ((slice(0, tall), re[:, tall:]), (slice(tall, 2 * tall), im[:, tall:])):
            block = block.reshape(2, nm, 2, hq, tall).astype(jnp.bfloat16)
            for h in range(2):
                for b in range(2):
                    stage[(i + h) % nt, :, 1 + b, h * hq : (h + 1) * hq, cols] = block[h, :, b]

    groups = ((0, 1), (1, 1), (2, 1), (3, 1), (1, 3))
    slots = (0, 1, 3, 2)

    def slot_of(i, j):
        return slots[i] * nm + j

    arrivals = (
        (0, 4, 1, nm - 1), (0, 1, nm, 2 * nm), (0, 1, 3 * nm, nm),
        (1, 1, nm, 2 * nm), (1, 1, 3 * nm, nm), (2, 1, nm, 3 * nm), (3, 1, nm, 3 * nm),
    )

    def awaited(g, i):
        return 0 if i == 0 else (1, 3, 5, 6)[g] + (1 if i == 2 and g < 2 else 0)

    def a_copy(g, i, j):
        v, n = groups[g]
        to = mom_at(j)
        return pltpu.make_async_remote_copy(
            src_ref=stage.at[i, share(to), pl.ds(v, n)],
            dst_ref=held.at[1, pl.ds(v, n), slot_of(i, j)],
            send_sem=a_send,
            recv_sem=a_recv.at[awaited(g, i)],
            device_id=dev(tile_at(i), to, z),
            device_id_type=MESH,
        )

    def own_copy():
        return pltpu.make_async_copy(stage.at[0, mine], held.at[1, pl.ds(0, 4), 0], own_sem)

    def send(g, i):
        for j in range(nm):
            if (i, j) != (0, 0):
                a_copy(g, i, j).start()

    def arrived(n):
        v, units, slot, many = arrivals[n]
        drained(held.at[1, pl.ds(v, units), pl.ds(slot, many)], a_recv.at[n])

    chunks = (
        (0, 1, 0, 1), (1, 3, 0, 1), (0, 3, 1, nm - 1),
        (0, 1, nm, 2 * nm), (0, 1, 3 * nm, nm),
        (1, 1, nm, 2 * nm), (1, 1, 3 * nm, nm), (2, 1, nm, 3 * nm), (3, 1, 1, 4 * nm - 1),
    )
    unit_of = (0, 4, 4, 0, 0, 1, 1, 2, 3)

    def z_copy(k, up):
        v, n, s, w = chunks[k]
        side = 0 if up else 1
        if s == 0:
            src, dst = stage.at[0, mine, pl.ds(v, n)], held.at[2 * side, pl.ds(v, n), 0]
        else:
            src, dst = held.at[1, pl.ds(v, n), pl.ds(s, w)], held.at[2 * side, pl.ds(v, n), pl.ds(s, w)]
        return pltpu.make_async_remote_copy(
            src_ref=src,
            dst_ref=dst,
            send_sem=z_send.at[side],
            recv_sem=z_recv.at[side, unit_of[k]],
            device_id=dev(t, up_mom if up else down_mom, z + 1 if up else z - 1),
            device_id_type=MESH,
        )

    def pass_on(k):
        @pl.when(has_up)
        def _():
            z_copy(k, True).start()

        @pl.when(has_down)
        def _():
            z_copy(k, False).start()

    base = lax.rem(ring, 2)
    near, far = lax.rem(base - ring + nt, nt), lax.rem(1 - base - ring + nt, nt)
    loads[0].wait()
    drained(g_ref.at[pl.ds(0, 2 * tall)], load_sem.at[0])
    scale_rows(near)
    put_cross(base)
    drained(g_ref.at[pl.ds(0, 2 * tall)], load_sem.at[1])
    scale_rows(far)
    put_cross(1 - base)
    pl.semaphore_wait(barrier, nt * nm - 1 + has_up.astype(jnp.int32) + has_down.astype(jnp.int32))
    pass_on(0)
    send(0, 0)
    send(0, 1)
    send(0, 3)
    send(0, 2)
    scale_rows(lax.rem(near + 2, nt))
    scale_rows(lax.rem(far + 2, nt))
    put_pair(0)
    put_pair(3)
    send(4, 0)
    pass_on(1)
    own_copy().start()
    put_pair(1)
    send(1, 1)
    put_pair(2)
    for g, i in ((1, 3), (1, 2), (2, 2), (2, 1), (2, 3), (3, 2), (3, 1), (3, 3)):
        send(g, i)
    for n in range(3):
        arrived(n)
        pass_on(2 + n)

    @pl.when(jnp.logical_not(has_down))
    def _():
        held[0] = jnp.zeros(held.shape[1:], held.dtype)

    @pl.when(jnp.logical_not(has_up))
    def _():
        held[2] = jnp.zeros(held.shape[1:], held.dtype)

    for copy in small:
        copy.wait()
    shifts = [lax.rem(lax.rem(shift_ref[s], nm) + nm, nm) for s in range(shift_ref.shape[0])]
    table = []
    for diff in range(nm):
        per_off = []
        for o in range(NW):
            acc = jnp.float32(0.0)
            for s in range(len(shifts)):
                acc = acc + jnp.where(shifts[s] == diff, coup_ref[s, o], 0.0)
            per_off.append(acc)
        row = []
        for d in range(2 * HW + 1):
            acc = jnp.float32(0.0)
            for o in range(NW):
                acc = acc + jnp.where(off_ref[o] + HW == d, per_off[o], 0.0)
            row.append(acc)
        table.append(row)
    for d in range(2 * HW + 1):
        tab[0, d] = 0.5 * (table[0][d] + table[1][d])
        tab[1, d] = 0.5 * (table[0][d] - table[1][d])

    for n in (3, 4):
        arrived(n)
        pass_on(2 + n)
    own_copy().wait()

    bases = []
    for p in range(nt):
        i = lax.rem(ring - order(p) + nt, nt)
        bases.append((i + (i // 2) * (5 - 2 * i)) * nm)

    def block_lo(block, who):
        return pl.multiple_of((block * nm + share(who)) * qr, qr)

    def pieces(v, who, here):
        if v == 0:
            block = ring // 2 if here else 1 - ring // 2
            return [(0, qr, 2, block_lo(block, who), 2, 2)]
        if v == 3:
            return [(3 * qr, qr, 3, block_lo(0, who), None, None)]
        off = (v - 1) * hq
        return [
            (v * qr + h * hq, hq, h, pl.multiple_of(block_lo(h, who) + off, hq), 1 - h, 1 if h == 0 else nt - 1)
            for h in range(2)
        ]

    def near_copy(v, h, kk, who):
        lo, n, slot, row, _, _ = pieces(v, who, True)[h]
        return pltpu.make_async_remote_copy(
            src_ref=fin.at[kk, :, pl.ds(lo, n)],
            dst_ref=parts.at[slot, :, pl.ds(row, n)],
            send_sem=near_send,
            recv_sem=mixed_recv.at[(v + 1) // 2],
            device_id=dev(t, mom_at(kk), z),
            device_id_type=MESH,
        )

    def far_copy(v, h, kk, who, here):
        lo, n, _, row, slot, step = pieces(v, who, here)[h]
        return pltpu.make_async_remote_copy(
            src_ref=fin.at[kk, :, pl.ds(lo, n)],
            dst_ref=parts.at[slot, :, pl.ds(row, n)],
            send_sem=far_send,
            recv_sem=mixed_recv.at[(v + 1) // 2],
            device_id=dev(tile_at(step), mom_at(kk), z),
            device_id_type=MESH,
        )

    def halves(v):
        return range(2 if v in (1, 2) else 1)

    def mix(v):
        for side, there in enumerate((has_down, has_up)):
            @pl.when(there)
            def _():
                got = held.at[2 * side]
                if v == 0:
                    drained(got.at[pl.ds(1, 3), pl.ds(0, nm)], z_recv.at[side, 4])
                first = (nm - 1 if v == 0 else nm, nm, nm, 1)[v]
                got = got.at[v, pl.ds(first, (3 * nm + 1, 3 * nm, 3 * nm, 4 * nm - 1)[v])]
                drained(got, z_recv.at[side, v])

        own = pieces(v, m, True)
        weight = [[tab[part, d] for d in range(2 * HW + 1)] for part in range(2)]
        wide = 2 * tall // LANES
        for lo, n, slot, row, _, _ in own:
            for step in range(n // PACK * wide):
                r = step // wide * PACK
                inner = pl.ds(lo - v * qr + r, PACK)
                rows = pl.ds(lo + r, PACK)
                cols = pl.ds(step % wide * LANES, LANES)
                acc = [[None] * nt for _ in range(2)]
                for zs in range(3):
                    for p in range(nt):
                        src = zs * nt + p
                        x = [held[zs, v, bases[p] + (j + zs + 1) % 2, inner, cols].astype(jnp.float32) for j in range(2)]
                        for part, y in enumerate((x[0] + x[1], x[0] - x[1])):
                            for e in range(nt):
                                if 0 <= src - e <= 2 * HW:
                                    term = weight[part][src - e] * y
                                    acc[part][e] = term if acc[part][e] is None else acc[part][e] + term
                for e in range(nt):
                    for kk, value in enumerate((acc[0][e] + acc[1][e], acc[0][e] - acc[1][e])):
                        value = value.astype(jnp.bfloat16)
                        if kk == 0:
                            parts[slot, e, pl.ds(pl.multiple_of(row + r, PACK), PACK), cols] = value
                        if kk > 0 or v < 3:
                            fin[kk, e, rows, cols] = value

        if v < 3:
            for h in halves(v):
                for kk in range(nm):
                    far_copy(v, h, kk, m, True).start()
        for h in halves(v):
            for kk in range(1, nm):
                near_copy(v, h, kk, m).start()

    def landed(n):
        copies, rows = ((2 * nm - 1, qr), (2 * nm - 1, 2 * qr), (nm - 1, qr))[n]
        drained(parts.at[pl.ds(0, copies), :, pl.ds(0, rows)], mixed_recv.at[n])

    def kept(tile):
        found = jnp.float32(0.0)
        for b in range(nbr_ref.shape[1]):
            found = jnp.where(nbr_ref[t, b] == tile, 1.0, found)
        return found

    def store(part, tile, flip):
        keep = kept(tile)

        for e in range(nt):
            re, im = parts[part, e, :, :tall].astype(jnp.float32), parts[part, e, :, tall:].astype(jnp.float32)
            if flip:
                re, im = re.T, -im.T
            re, im = (re * keep).astype(jnp.bfloat16), (im * keep).astype(jnp.bfloat16)
            out_ref[e, :, pl.ds(pl.multiple_of(tile * tall, tall), tall)] = re
            out_ref[e, :, pl.ds(pl.multiple_of(orb + tile * tall, tall), tall)] = im

    def store_diagonal():
        row, col = triangle()
        keep = kept(t)

        for e in range(nt):
            packed = [
                parts[3, e, c * qr : (c + 1) * qr, h * tall : (h + 1) * tall] for c in range(nm) for h in range(2)
            ]
            both = jnp.concatenate(packed, axis=0).astype(jnp.float32)
            turned = both.T
            re = jnp.where(row > col, turned, both)
            im = jnp.where(row > col, both, jnp.where(row < col, -turned, 0.0))
            out_ref[e, :, pl.ds(pl.multiple_of(t * tall, tall), tall)] = (re * keep).astype(jnp.bfloat16)
            out_ref[e, :, pl.ds(pl.multiple_of(orb + t * tall, tall), tall)] = (im * keep).astype(jnp.bfloat16)

    arrived(5)
    pass_on(7)
    arrived(6)
    pass_on(8)
    mix(0)
    drained(held.at[1, pl.ds(0, 4), pl.ds(0, nt * nm - 1)], a_send)
    for v in range(1, 4):
        mix(v)
    landed(0)

    @pl.when(ring < 2)
    def _():
        store(2, tile_at(2), False)

    @pl.when(ring >= 2)
    def _():
        store(2, tile_at(2), True)

    for side, there in enumerate((has_up, has_down)):
        @pl.when(there)
        def _():
            drained(held.at[1], z_send.at[side])

    drained(fin.at[:, :, pl.ds(0, 3 * qr)], far_send)
    landed(2)
    store_diagonal()
    drained(fin.at[pl.ds(1, nm - 1)], near_send)
    landed(1)
    store(1, tile_at(nt - 1), True)
    store(0, tile_at(1), False)


def fused(green_ret, injection, mom_shift, phon_off, coupling, tile_nbr):
    nt, nm, nz = lax.axis_size("tile"), lax.axis_size("mom"), lax.axis_size("ewin")
    orbitals, width = green_ret.shape[3:]
    tall = orbitals // nt
    qr = tall // nm // 2
    green = green_ret.reshape(orbitals, width)
    gamma = injection.reshape(1, orbitals)
    vmem, anywhere = pl.BlockSpec(memory_space=pltpu.VMEM), pl.BlockSpec(memory_space=pl.ANY)
    args = (green, gamma, mom_shift, phon_off, coupling, tile_nbr)
    dma = pltpu.SemaphoreType.DMA
    total = pl.pallas_call(
        lambda *refs: fused_kernel(nt, nm, nz, *refs),
        out_shape=pltpu.VMEM((nt, tall, width), jnp.bfloat16),
        in_specs=[anywhere] * len(args),
        out_specs=vmem,
        scratch_shapes=[
            pltpu.VMEM(green.shape, green.dtype),
            pltpu.VMEM(gamma.shape, gamma.dtype),
            *[pltpu.SMEM(a.shape, a.dtype) for a in args[2:]],
            pltpu.VMEM((nt, 2 * tall, width), jnp.bfloat16),
            pltpu.VMEM((nt, nm, 4, qr, 2 * tall), jnp.bfloat16),
            pltpu.VMEM((3, 4, nt * nm, qr, 2 * tall), jnp.bfloat16),
            pltpu.VMEM((nm, nt, 4 * qr, 2 * tall), jnp.bfloat16),
            pltpu.VMEM((4, nt, tall, 2 * tall), jnp.bfloat16),
            pltpu.SMEM((nm, 2 * HW + 1), jnp.float32),
            dma((7,)),
            dma,
            dma((7,)),
            dma((2,)),
            dma((2, 5)),
            dma,
            dma,
            dma((3,)),
            dma,
        ],
        compiler_params=pltpu.CompilerParams(collective_id=0, has_side_effects=True),
    )(*args)
    return total[None, None]


def with_halo(shard, sides, width):
    for axis, dim in sides:
        peers, length = (lax.axis_size(axis), shard.shape[dim])
        up = [(i, (i + 1) % peers) for i in range(peers - 1)]
        down = [(j, i) for i, j in up]
        last = lax.slice_in_dim(shard, length - width, length, axis=dim)
        initial = lax.slice_in_dim(shard, 0, width, axis=dim)
        before = lax.ppermute(last, axis, up)
        after = lax.ppermute(initial, axis, down)
        shard = jnp.concatenate([before, shard, after], axis=dim)
    return shard


def on_device(green_ret, injection, mom_shift, phon_off, coupling, tile_nbr):
    blocks = green_ret[0, 0]
    gamma = injection[0, 0]
    orbitals = blocks.shape[1]
    ntiles = lax.axis_size("tile")
    per_tile = orbitals // ntiles
    real_part = blocks[:, :, :orbitals].astype(jnp.float32)
    imag_part = blocks[:, :, orbitals:].astype(jnp.float32)
    scale = gamma[:, None, :]
    left_re = jnp.concatenate([real_part * scale, imag_part * scale], axis=2).astype(jnp.bfloat16)
    left_im = jnp.concatenate([imag_part * scale, -real_part * scale], axis=2).astype(jnp.bfloat16)
    real_out = jnp.einsum("prk,pck->prc", left_re, blocks, preferred_element_type=jnp.float32)
    imag_out = jnp.einsum("prk,pck->prc", left_im, blocks, preferred_element_type=jnp.float32)
    payload = jnp.concatenate([real_out, imag_out], axis=2).astype(jnp.bfloat16)
    exchanged = lax.all_to_all(payload, "tile", split_axis=1, concat_axis=0, tiled=True)
    energies = exchanged.shape[0]
    rimmed = with_halo(exchanged, (("ewin", 0),), HW)
    extended = lax.all_gather(rimmed[None], "mom", axis=0, tiled=True)
    nmom = lax.axis_size("mom")
    here = lax.axis_index("mom")
    source = jnp.mod(here - mom_shift, nmom)
    onehot = (source[:, None] == jnp.arange(nmom, dtype=jnp.int32)[None, :]).astype(jnp.float32)
    weights = jnp.dot(onehot.T, coupling, precision=lax.Precision.HIGHEST)
    total = jnp.zeros(exchanged.shape, jnp.float32)
    for offset in range(NW):
        start = HW + phon_off[offset]
        piece = lax.dynamic_slice_in_dim(extended, start, energies, 1)
        for moment in range(nmom):
            total = total + weights[moment, offset] * piece[moment].astype(jnp.float32)
    tile_here = lax.axis_index("tile")
    neighbours = lax.dynamic_index_in_dim(tile_nbr, tile_here, 0, keepdims=False)
    coltile = jnp.arange(orbitals, dtype=jnp.int32) // per_tile
    colmask = jnp.any(coltile[:, None] == neighbours[None, :], axis=1).astype(jnp.float32)
    colmask = jnp.concatenate([colmask, colmask])
    result = (total * colmask[None, None, :]).astype(jnp.bfloat16)
    return result[None, None]


def body_for(mesh):
    nt, nm = mesh.shape["tile"], mesh.shape["mom"]

    def body(green_ret, *rest):
        points, orbitals = green_ret.shape[2:4]
        aligned = orbitals % (nt * LANES) == 0 and orbitals % (nt * nm * 4 * PACK) == 0
        if aligned and points == 1 and nt == HW and nm == 2:
            return fused(green_ret, *rest)
        return on_device(green_ret, *rest)

    return body


def solution(mesh):
    placed = (
        P("mom", "ewin", "tile", None, None),
        P("mom", "ewin", "tile", None),
        P(),
        P(),
        P(),
        P(),
    )
    return jax.shard_map(
        body_for(mesh),
        mesh=mesh,
        in_specs=placed,
        out_specs=P("mom", "ewin", None, "tile", None),
        check_vma=False,
    )
```
